256 devices in a mesh: band: 32 (over x_lo, z, core), dom: 8 (over x_hi, y).
Axes of the slice: x: 4 (x_hi: 2, x_lo: 2; x = x_hi * 2 + x_lo), y: 4, z: 8, core: 2. Of those that a mesh axis runs over, the one named last changes fastest.
Arguments:
- states: float32 [64, 192, 64, 256], P('band', 'dom'), may hold values from -6 to 6
- potential: float32 [192, 64, 256], P('dom'), may hold values from 0 to 2
- rotation_panel: float32 [2, 64], P(None, 'band'), may hold values from -4 to 4
- owner: int32 [1], replicated, may hold values from 0 to 31
Outputs:
- rotated: float32 [64, 192, 64, 256], P('band', 'dom')
The draws below stay inside these ranges and needn't reach their ends.
Inputs may be any that keep to these rules, and one draw needn't show every extreme that they name: owner is the index of one block of 2 states along the band axis.
All inputs are finite; a program needn't handle non-finite values.
Results may differ from the reference program's by a relative error of at most 0.00017.
Values sent between devices are 32-bit elements; how exact they have to be, the bound alone decides.
No kernel may reach another device: no remote copies, remote signals or barrier semaphores. Data moves between devices by JAX's collectives and lax.ppermute only.
A program may use at most 128 MiB of HBM per device.

```python
import jax
import jax.numpy as jnp
from jax import lax

SB = 2
NY = 64
NZ = 256
DEG = 4
STATES = 64
NX = 192
N_BAND = 32


def level_of(key, dims, split, smallest, largest):
    def one(position, blocks):
        heights = jax.random.uniform(jax.random.fold_in(jax.random.fold_in(key, 6), position), (blocks,), jnp.float32, smallest / len(split), largest / len(split))
        return jnp.repeat(jnp.exp(heights), dims[position] // blocks).reshape((-1,) + (1,) * (len(dims) - position - 1))

    factor_of = one(*split[0])
    for cut in split[1:]:
        factor_of = factor_of * one(*cut)
    return factor_of


def bell_draw(own_key, shape, width, bound, split=(), held_as=jnp.bfloat16):
    loudness = level_of(own_key, shape, split, -0.22, 0.18) if split else 1.0
    drawn = jax.random.normal(own_key, shape, jnp.float32) * width * loudness
    return jnp.minimum(jnp.maximum(drawn, -bound), bound).astype(held_as)


def setup_inputs(seed: int = 0) -> dict:
    key_list = jax.random.split(jax.random.key(seed), 5)
    states = bell_draw(key_list[0], (STATES, NX, NY, NZ), 1.0, 6.0, ((0, 32), (1, 8)), jnp.float32)
    potential = jnp.clip(2.0 * jax.random.uniform(key_list[1], (NX, NY, NZ), jnp.float32) ** level_of(key_list[1], (NX, NY, NZ), ((0, 8),), -0.2, 0.2), 0.0, 2.0)
    rotation_panel = bell_draw(key_list[2], (SB, STATES), SB ** -0.5, 4.0, ((1, 32),), jnp.float32)
    owner = jax.random.randint(key_list[3], (1,), 0, N_BAND).astype(jnp.int32)
    return dict(states=states, potential=potential, rotation_panel=rotation_panel, owner=owner)


stencil_weights = (-5369.0 / 1800.0, 12.0 / 7.0, -15.0 / 56.0, 10.0 / 189.0, -1.0 / 112.0, 2.0 / 1925.0, -1.0 / 16632.0)
center_value = 8.0
half_width = 5.0


def scaled_apply(padded, potential):
    length = potential.shape[0]
    middle = padded[:, 6:6 + length]
    along = (3.0 * stencil_weights[0]) * middle
    for offset in range(1, 7):
        along = along + stencil_weights[offset] * (padded[:, 6 + offset:6 + offset + length] + padded[:, 6 - offset:6 - offset + length])
    side = jnp.pad(middle, ((0, 0), (0, 0), (6, 6), (6, 6)))
    size_y = middle.shape[2]
    size_z = middle.shape[3]
    for offset in range(1, 7):
        pair_y = side[:, :, 6 + offset:6 + offset + size_y, 6:6 + size_z] + side[:, :, 6 - offset:6 - offset + size_y, 6:6 + size_z]
        pair_z = side[:, :, 6:6 + size_y, 6 + offset:6 + offset + size_z] + side[:, :, 6:6 + size_y, 6 - offset:6 - offset + size_z]
        along = along + stencil_weights[offset] * (pair_y + pair_z)
    applied = -0.5 * along + potential * middle
    return (applied - center_value * middle) / half_width


def reference(states, potential, rotation_panel, owner):
    def pad_x(value):
        return jnp.pad(value, ((0, 0), (6, 6), (0, 0), (0, 0)))

    def filter_block(block):
        previous = block
        current = scaled_apply(pad_x(block), potential)
        for step in range(DEG - 1):
            following = 2.0 * scaled_apply(pad_x(current), potential) - previous
            previous = current
            current = following
        return current

    blocks = states.reshape(N_BAND, SB, NX, NY, NZ)
    filtered = lax.map(filter_block, blocks)
    panel = lax.dynamic_index_in_dim(filtered, owner[0].astype(jnp.int32), 0, keepdims=False)
    mixed = jnp.einsum('sxyz,st->txyz', panel, rotation_panel, precision=lax.Precision.HIGHEST)
    return filtered.reshape(STATES, NX, NY, NZ) + mixed
```

```python
import jax
import jax.numpy as jnp
import ml_dtypes
import numpy as np
from jax import lax
from jax.experimental import pallas as pl
from jax.experimental.pallas import tpu as pltpu
from jax.sharding import PartitionSpec as P

DEG = 4
RIM = 6
WEIGHTS = (
    -5369.0 / 1800.0,
    12.0 / 7.0,
    -15.0 / 56.0,
    10.0 / 189.0,
    -1.0 / 112.0,
    2.0 / 1925.0,
    -1.0 / 16632.0,
)
CENTER = 8.0
HALF_WIDTH = 5.0
LAPLACE = -1.0 / HALF_WIDTH
SLOPE = 2.0 / HALF_WIDTH
SHIFT = -2.0 * CENTER / HALF_WIDTH + LAPLACE * 3.0 * WEIGHTS[0]
SPAN = [LAPLACE * w for w in WEIGHTS]
GROUP = 4


def band_matrix(size, copies):
    one = np.zeros((size, size), np.float64)
    for offset in range(1, RIM + 1):
        one += SPAN[offset] * (np.eye(size, k=offset) + np.eye(size, k=-offset))
    return np.kron(np.eye(copies), one).astype(np.float32)


def halves(matrix):
    high = matrix.astype(ml_dtypes.bfloat16)
    low = (matrix - high.astype(np.float32)).astype(ml_dtypes.bfloat16)
    return high, low


def step_kernel(first, *refs):
    if first:
        y_ref, below_ref, above_ref, pot_ref, mz_ref, my_ref = refs[:6]
        prev_ref = None
        next_ref, low_ref, high_ref = refs[6:]
    else:
        y_ref, below_ref, above_ref, prev_ref, pot_ref, mz_ref, my_ref = refs[:7]
        next_ref, low_ref, high_ref = refs[7:]
    planes, rows, lanes = y_ref.shape

    def along_plane(g, carry):
        at = pl.multiple_of(g * GROUP, GROUP)
        block = y_ref[pl.ds(at, GROUP)].reshape(GROUP * rows, lanes)
        high = block.astype(jnp.bfloat16)
        low = (block - high.astype(jnp.float32)).astype(jnp.bfloat16)
        total = jnp.dot(
            jnp.concatenate([high, high, low], axis=1),
            mz_ref[...],
            preferred_element_type=jnp.float32,
        )
        total = total + jnp.dot(
            my_ref[...],
            jnp.concatenate([high, low, high], axis=0),
            preferred_element_type=jnp.float32,
        )
        next_ref[pl.ds(at, GROUP)] = total.reshape(GROUP, rows, lanes)
        return carry

    lax.fori_loop(0, planes // GROUP, along_plane, 0)

    def across_planes(i, carry):
        row = pl.ds(pl.multiple_of(i * 8, 8), 8)
        for j in range(lanes // 128):
            col = pl.ds(j * 128, 128)
            line = [below_ref[p, row, col] for p in range(RIM)]
            line += [y_ref[p, row, col] for p in range(planes)]
            line += [above_ref[p, row, col] for p in range(RIM)]
            for p in range(planes):
                total = next_ref[p, row, col]
                for offset in range(1, RIM + 1):
                    total = total + SPAN[offset] * (
                        line[p + RIM - offset] + line[p + RIM + offset]
                    )
                total = total + (SLOPE * pot_ref[p, row, col] + SHIFT) * line[p + RIM]
                total = 0.5 * total if first else total - prev_ref[p, row, col]
                next_ref[p, row, col] = total
                if p < RIM:
                    low_ref[p, row, col] = total
                if p >= planes - RIM:
                    high_ref[p - (planes - RIM), row, col] = total
        return carry

    lax.fori_loop(0, rows // 8, across_planes, 0)


def step(first, y, below, above, prev, potential, mz, my):
    import functools

    args = [y, below, above] + ([] if first else [prev]) + [potential, mz, my]
    vmem = pl.BlockSpec(memory_space=pltpu.VMEM)
    rim = jax.ShapeDtypeStruct((RIM,) + y.shape[1:], jnp.float32)
    return pl.pallas_call(
        functools.partial(step_kernel, first),
        out_shape=(jax.ShapeDtypeStruct(y.shape, jnp.float32), rim, rim),
        in_specs=[vmem] * len(args),
        out_specs=(vmem, vmem, vmem),
        compiler_params=pltpu.CompilerParams(vmem_limit_bytes=32 * 1024 * 1024),
        name="chebyshev_first" if first else "chebyshev_step",
    )(*args)


def on_device(states, potential, rotation_panel, owner):
    size = lax.axis_size("dom")
    up = [(i, i + 1) for i in range(size - 1)]
    down = [(j, i) for i, j in up]
    bands = lax.axis_size("band")
    depth = bands // 4
    planes, rows, lanes = states.shape[1:]

    def device(x, z, c):
        return (x * depth + z % depth) * 2 + c

    chips = [(x, z, c) for x in range(2) for z in range(depth) for c in range(2)]
    swap_core = [(device(x, z, c), device(x, z, 1 - c)) for x, z, c in chips]
    swap_x = [(device(x, z, c), device(1 - x, z, c)) for x, z, c in chips]
    columns = [[device(x, z, c) for z in range(depth)] for x in range(2) for c in range(2)]

    mz_high, mz_low = halves(band_matrix(lanes, 1))
    my_high, my_low = halves(band_matrix(rows, GROUP))
    mz = jnp.asarray(np.concatenate([mz_high, mz_low, mz_high], axis=0))
    my = jnp.asarray(np.concatenate([my_high, my_high, my_low], axis=1))

    def rims(low, high):
        return lax.ppermute(high, "dom", up), lax.ppermute(low, "dom", down)

    count = states.shape[0]
    current = [states[s] for s in range(count)]
    previous = [None] * count
    edges = [(c[:RIM], c[planes - RIM :]) for c in current]
    for k in range(DEG):
        for s in range(count):
            below, above = rims(*edges[s])
            following, low, high = step(
                k == 0, current[s], below, above, previous[s], potential, mz, my
            )
            previous[s], current[s] = current[s], following
            edges[s] = (low, high)

    me = lax.axis_index("band")
    source = owner[0]
    near_core = (me % 2) == (source % 2)
    near_x = (me // (2 * depth)) == (source // (2 * depth))
    source_z = (source // 2) % depth

    def spread(block):
        shape = block.shape
        block = block.reshape(2, 2, depth, -1, lanes)
        half = jnp.where(near_core, block[0], lax.ppermute(block[1], "band", swap_core))
        quarter = jnp.where(near_x, half[0], lax.ppermute(half[1], "band", swap_x))
        pieces = lax.all_to_all(quarter, "band", 0, 0, axis_index_groups=columns)
        piece = lax.dynamic_index_in_dim(pieces, source_z, 0, keepdims=False)
        quarter = lax.all_gather(piece, "band", axis=0, axis_index_groups=columns)
        other = lax.ppermute(quarter, "band", swap_x)
        half = jnp.stack([jnp.where(near_x, quarter, other), jnp.where(near_x, other, quarter)])
        other = lax.ppermute(half, "band", swap_core)
        whole = jnp.stack([jnp.where(near_core, half, other), jnp.where(near_core, other, half)])
        return whole.reshape(shape)

    panel = [spread(c) for c in current]
    rotated = []
    for t in range(count):
        total = current[t]
        for s in range(count):
            total = total + rotation_panel[s, t] * panel[s]
        rotated.append(total)
    return jnp.stack(rotated)


def solution(mesh):
    in_specs = (P("band", "dom", None, None), P("dom", None, None), P(None, "band"), P())
    out_specs = P("band", "dom", None, None)
    return jax.shard_map(
        on_device, mesh=mesh, in_specs=in_specs, out_specs=out_specs, check_vma=False
    )
```

```python
import functools

import jax
import jax.numpy as jnp
import ml_dtypes
import numpy as np
from jax import lax
from jax.experimental import pallas as pl
from jax.experimental.pallas import tpu as pltpu
from jax.sharding import PartitionSpec as P

DEG = 4
RIM = 6
WEIGHTS = (
    -5369.0 / 1800.0,
    12.0 / 7.0,
    -15.0 / 56.0,
    10.0 / 189.0,
    -1.0 / 112.0,
    2.0 / 1925.0,
    -1.0 / 16632.0,
)
CENTER = 8.0
HALF_WIDTH = 5.0
LAPLACE = -1.0 / HALF_WIDTH
SLOPE = 2.0 / HALF_WIDTH
SHIFT = -2.0 * CENTER / HALF_WIDTH + LAPLACE * 3.0 * WEIGHTS[0]
SPAN = [LAPLACE * w for w in WEIGHTS]
GROUP = 4


def band_matrix(size, copies):
    one = np.zeros((size, size), np.float64)
    for offset in range(1, RIM + 1):
        one += SPAN[offset] * (np.eye(size, k=offset) + np.eye(size, k=-offset))
    return np.kron(np.eye(copies), one).astype(np.float32)


def halves(matrix):
    high = matrix.astype(ml_dtypes.bfloat16)
    low = (matrix - high.astype(np.float32)).astype(ml_dtypes.bfloat16)
    return high, low


def step_kernel(first, place_ref, *refs):
    if first:
        y_ref, odd_ref, even_ref, pot_ref, mz_ref, my_ref = refs[:6]
        prev_ref = None
        refs = refs[6:]
    else:
        y_ref, odd_ref, even_ref, prev_ref, pot_ref, mz_ref, my_ref = refs[:7]
        refs = refs[7:]
    next_ref, near_ref, far_ref, below_ref, above_ref = refs[1:]
    planes, rows, lanes = y_ref.shape
    place = place_ref[0]
    even = (place & 1) == 0
    last = place_ref[1]
    zero = jnp.zeros((rows, lanes), jnp.float32)
    for p in range(RIM):
        one, two = odd_ref[p], even_ref[p]
        below_ref[p] = jnp.where(place == 0, zero, jnp.where(even, two, one))
        above_ref[p] = jnp.where(place == last, zero, jnp.where(even, one, two))

    def along_plane(g, carry):
        group = pl.ds(pl.multiple_of(g * GROUP, GROUP), GROUP)
        block = y_ref[group].reshape(GROUP * rows, lanes)
        high = block.astype(jnp.bfloat16)
        low = (block - high.astype(jnp.float32)).astype(jnp.bfloat16)
        total = jnp.dot(
            jnp.concatenate([high, high, low], axis=1),
            mz_ref[...],
            preferred_element_type=jnp.float32,
        )
        total = total + jnp.dot(
            my_ref[...],
            jnp.concatenate([high, low, high], axis=0),
            preferred_element_type=jnp.float32,
        )
        next_ref[group] = total.reshape(GROUP, rows, lanes)
        return carry

    lax.fori_loop(0, planes // GROUP, along_plane, 0, unroll=2)

    def across_planes(i, carry):
        row = pl.ds(pl.multiple_of(i * 8, 8), 8)
        for j in range(lanes // 128):
            col = pl.ds(j * 128, 128)
            line = [below_ref[p, row, col] for p in range(RIM)]
            line += [y_ref[p, row, col] for p in range(planes)]
            line += [above_ref[p, row, col] for p in range(RIM)]
            for p in range(planes):
                here = p + RIM
                out = next_ref[p, row, col]
                for offset in range(1, RIM + 1):
                    out = out + SPAN[offset] * (line[here - offset] + line[here + offset])
                out = out + (SLOPE * pot_ref[p, row, col] + SHIFT) * line[here]
                next_ref[p, row, col] = 0.5 * out if first else out - prev_ref[p, row, col]
        return carry

    lax.fori_loop(0, rows // 8, across_planes, 0)

    @pl.when(even)
    def _():
        near_ref[...] = next_ref[planes - RIM :]
        far_ref[...] = next_ref[:RIM]

    @pl.when(jnp.logical_not(even))
    def _():
        near_ref[...] = next_ref[:RIM]
        far_ref[...] = next_ref[planes - RIM :]


def step(first, place, y, one, two, prev, potential, mz, my, token):
    args = [y, one, two] + ([] if first else [prev]) + [potential, mz, my]
    vmem = pl.BlockSpec(memory_space=pltpu.VMEM)
    rim = jax.ShapeDtypeStruct((RIM,) + y.shape[1:], jnp.float32)
    return pl.pallas_call(
        functools.partial(step_kernel, first),
        out_shape=(jax.ShapeDtypeStruct(y.shape, jnp.float32), rim, rim),
        in_specs=[pl.BlockSpec(memory_space=pltpu.SMEM)] + [vmem] * len(args)
        + [pl.BlockSpec(memory_space=pl.ANY)],
        out_specs=(vmem, vmem, vmem),
        scratch_shapes=[pltpu.VMEM(rim.shape, jnp.float32)] * 2,
        compiler_params=pltpu.CompilerParams(vmem_limit_bytes=8 * 1024 * 1024),
        name="chebyshev_first" if first else "chebyshev_step",
    )(place, *args, token)


def mix_kernel(count, spots_ref, turn_ref, *refs):
    own, parts, out_ref = refs[:count], refs[count:-1], refs[-1]
    quarters = len(parts) // count
    width, rows, lanes = parts[0].shape
    for k in range(quarters):
        spot = spots_ref[k]
        for p in range(width):
            for i in range(rows // 8):
                row = slice(i * 8, i * 8 + 8)
                panel = [parts[s * quarters + k][p, row, :] for s in range(count)]
                for t in range(count):
                    total = own[t][spot + p, row, :]
                    for s in range(count):
                        total = total + turn_ref[s, t] * panel[s]
                    out_ref[t, spot + p, row, :] = total


def mix(spots, turn, own, parts):
    vmem = pl.BlockSpec(memory_space=pltpu.VMEM)
    smem = pl.BlockSpec(memory_space=pltpu.SMEM)
    count = len(own)
    shape = (count,) + own[0].shape
    return pl.pallas_call(
        functools.partial(mix_kernel, count),
        out_shape=jax.ShapeDtypeStruct(shape, jnp.float32),
        in_specs=[smem, smem] + [vmem] * (len(own) + len(parts)),
        out_specs=vmem,
        compiler_params=pltpu.CompilerParams(vmem_limit_bytes=8 * 1024 * 1024),
        name="mix",
    )(spots, turn, *own, *parts)


def on_device(states, potential, rotation_panel, owner):
    size = lax.axis_size("dom")
    pairs = [(i, i ^ 1) for i in range(size)]
    others = [(i, (i + 1) % size if i % 2 else (i - 1) % size) for i in range(size)]
    depth = lax.axis_size("band") // 4
    count, planes, rows, lanes = states.shape

    def device(x, z, c):
        return (x * depth + z) * 2 + c

    chips = [(x, z, c) for x in range(2) for z in range(depth) for c in range(2)]
    swap_core = [(device(x, z, c), device(x, z, 1 - c)) for x, z, c in chips]
    swap_x = [(device(x, z, c), device(1 - x, z, c)) for x, z, c in chips]

    mz_high, mz_low = halves(band_matrix(lanes, 1))
    my_high, my_low = halves(band_matrix(rows, GROUP))
    mz = jnp.asarray(np.concatenate([mz_high, mz_low, mz_high], axis=0))
    my = jnp.asarray(np.concatenate([my_high, my_high, my_low], axis=1))

    slab = lax.axis_index("dom")
    place = jnp.stack([slab, jnp.int32(size - 1)])
    even = (slab & 1) == 0
    current = [states[s] for s in range(count)]
    previous = [None] * count
    edges = []
    token = potential
    for c in current:
        low, high = c[:RIM], c[planes - RIM :]
        edges.append((jnp.where(even, high, low), jnp.where(even, low, high)))
    me = lax.axis_index("band")
    source = owner[0]
    away = me ^ source
    core_off = away & 1
    x_off = jnp.where(away >= 2 * depth, 1, 0)
    source_z = (source >> 1) & (depth - 1)
    width = planes // 4
    spots = jnp.stack([((core_off ^ c) * 2 + (x_off ^ x)) * width for c in (0, 1) for x in (0, 1)])

    def split(block):
        got = lax.ppermute(block[2 * width :], "band", swap_core)
        return jnp.where(core_off == 0, block[: 2 * width], got)

    half = [None] * count
    for k in range(DEG):
        for s in range(count):
            one = lax.ppermute(edges[s][0], "dom", pairs)
            two = lax.ppermute(edges[s][1], "dom", others)
            if k == DEG - 1 and s == count - 1:
                ready, one, two = lax.optimization_barrier((ready, one, two))
            following, near, far = step(
                k == 0, place, current[s], one, two, previous[s], potential, mz, my, token
            )
            token = near
            previous[s], current[s] = current[s], following
            edges[s] = (near, far)
            if k == DEG - 1 and s == count - 1:
                half[0] = split(ready)
                half[s] = split(following)
            ready = following

    far_z = ((me >> 1) - source_z) & (depth - 1)
    rising = far_z <= depth // 2
    hops = jnp.where(rising, far_z, depth - far_z)
    ring = [(device(x, z, c), device(x, (z + 1) % depth, c)) for x, z, c in chips]
    back = [(j, i) for i, j in ring]

    chunks = []
    for s in range(count):
        got = lax.ppermute(half[s][width:], "band", swap_x)
        quarter = jnp.where(x_off == 0, half[s][:width], got)
        chunks += [quarter[: width // 2], quarter[width // 2 :]]
    last = len(chunks) + depth // 2
    stages = [chunks[0]]
    for stage in range(1, last):
        here = stages[-1]
        up = lax.ppermute(here, "band", ring)
        down = lax.ppermute(here, "band", back)
        here = jnp.where(rising, up, down)
        if stage < len(chunks):
            here = jnp.where(hops == 0, chunks[stage], here)
        stages.append(here)

    def arrived(c):
        out = stages[c]
        for h in range(1, depth // 2 + 1):
            out = jnp.where(hops == h, stages[c + h], out)
        return out

    parts = []
    for s in range(count):
        here = jnp.concatenate([arrived(2 * s), arrived(2 * s + 1)])
        there = lax.ppermute(here, "band", swap_x)
        parts += [
            here,
            there,
            lax.ppermute(here, "band", swap_core),
            lax.ppermute(there, "band", swap_core),
        ]
    return mix(spots, rotation_panel, current, parts)


def solution(mesh):
    in_specs = (P("band", "dom", None, None), P("dom", None, None), P(None, "band"), P())
    out_specs = P("band", "dom", None, None)
    return jax.shard_map(
        on_device, mesh=mesh, in_specs=in_specs, out_specs=out_specs, check_vma=False
    )
```

```python
import functools

import jax
import jax.numpy as jnp
import ml_dtypes
import numpy as np
from jax import lax
from jax.experimental import pallas as pl
from jax.experimental.pallas import tpu as pltpu
from jax.sharding import PartitionSpec as P

DEG = 4
RIM = 6
WEIGHTS = (
    -5369.0 / 1800.0,
    12.0 / 7.0,
    -15.0 / 56.0,
    10.0 / 189.0,
    -1.0 / 112.0,
    2.0 / 1925.0,
    -1.0 / 16632.0,
)
CENTER = 8.0
HALF_WIDTH = 5.0
LAPLACE = -1.0 / HALF_WIDTH
SLOPE = 2.0 / HALF_WIDTH
SHIFT = -2.0 * CENTER / HALF_WIDTH + LAPLACE * 3.0 * WEIGHTS[0]
SPAN = [LAPLACE * w for w in WEIGHTS]
GROUP = 4


def band_matrix(size, copies):
    one = np.zeros((size, size), np.float64)
    for offset in range(1, RIM + 1):
        one += SPAN[offset] * (np.eye(size, k=offset) + np.eye(size, k=-offset))
    return np.kron(np.eye(copies), one).astype(np.float32)


def halves(matrix):
    high = matrix.astype(ml_dtypes.bfloat16)
    low = (matrix - high.astype(np.float32)).astype(ml_dtypes.bfloat16)
    return high, low


def second_differences(planes, y_ref, below_ref, above_ref, pot_ref, mz_ref, my_ref, prev_ref, next_ref):
    rows, lanes = y_ref.shape[1:]

    def along_plane(g, carry):
        group = pl.ds(pl.multiple_of(g * GROUP, GROUP), GROUP)
        block = y_ref[group].reshape(GROUP * rows, lanes)
        high = block.astype(jnp.bfloat16)
        low = (block - high.astype(jnp.float32)).astype(jnp.bfloat16)
        total = jnp.dot(
            jnp.concatenate([high, high, low], axis=1),
            mz_ref[...],
            preferred_element_type=jnp.float32,
        )
        total = total + jnp.dot(
            my_ref[...],
            jnp.concatenate([high, low, high], axis=0),
            preferred_element_type=jnp.float32,
        )
        next_ref[group] = total.reshape(GROUP, rows, lanes)
        return carry

    lax.fori_loop(0, planes // GROUP, along_plane, 0, unroll=2)

    def across_planes(i, carry):
        row = pl.ds(pl.multiple_of(i * 8, 8), 8)
        for j in range(lanes // 128):
            col = pl.ds(j * 128, 128)
            line = [below_ref[p, row, col] for p in range(RIM)]
            line += [y_ref[p, row, col] for p in range(planes)]
            line += [above_ref[p, row, col] for p in range(RIM)]
            for p in range(planes):
                here = p + RIM
                out = next_ref[p, row, col]
                for offset in range(1, RIM + 1):
                    out = out + SPAN[offset] * (line[here - offset] + line[here + offset])
                out = out + (SLOPE * pot_ref[p, row, col] + SHIFT) * line[here]
                if prev_ref is None:
                    next_ref[p, row, col] = 0.5 * out
                else:
                    next_ref[p, row, col] = out - prev_ref[p, row, col]
        return carry

    lax.fori_loop(0, rows // 8, across_planes, 0)


def step_kernel(first, final, place_ref, *refs):
    y_ref, odd_ref, even_ref = refs[:3]
    prev_ref = None if first else refs[3]
    refs = refs[3:] if first else refs[4:]
    pot_ref, mz_ref, my_ref, token_ref = refs[:4]
    below_ref, above_ref = refs[-2:]
    planes, rows, lanes = y_ref.shape
    place = place_ref[0]
    even = (place & 1) == 0
    last = place_ref[1]
    zero = jnp.zeros((rows, lanes), jnp.float32)
    for p in range(RIM):
        one, two = odd_ref[p], even_ref[p]
        below_ref[p] = jnp.where(place == 0, zero, jnp.where(even, two, one))
        above_ref[p] = jnp.where(place == last, zero, jnp.where(even, one, two))
    use = (y_ref, below_ref, above_ref, pot_ref, mz_ref, my_ref, prev_ref)

    if final:
        out_ref, next_ref, sems = refs[4:7]
        copies = [pltpu.make_async_copy(token_ref, out_ref.at[0], sems.at[0])]
        copies += [pltpu.make_async_copy(next_ref, out_ref.at[1], sems.at[1])]
        copies[0].start()
        second_differences(planes, *use, next_ref)
        copies[1].start()
        copies[0].wait()
        copies[1].wait()
        return

    next_ref = refs[4]
    second_differences(planes, *use, next_ref)
    if len(refs) == 7:
        return
    near_ref, far_ref = refs[5:7]

    @pl.when(even)
    def _():
        near_ref[...] = next_ref[planes - RIM :]
        far_ref[...] = next_ref[:RIM]

    @pl.when(jnp.logical_not(even))
    def _():
        near_ref[...] = next_ref[:RIM]
        far_ref[...] = next_ref[planes - RIM :]


def step(k, final, place, y, one, two, prev, potential, mz, my, token):
    first = k == 0
    args = [y, one, two] + ([] if first else [prev]) + [potential, mz, my]
    vmem = pl.BlockSpec(memory_space=pltpu.VMEM)
    hbm = pl.BlockSpec(memory_space=pl.ANY)
    rim = jax.ShapeDtypeStruct((RIM,) + y.shape[1:], jnp.float32)
    whole = jax.ShapeDtypeStruct(y.shape, jnp.float32)
    scratch = [pltpu.VMEM(rim.shape, jnp.float32)] * 2
    if final:
        shapes, specs = jax.ShapeDtypeStruct((2,) + y.shape, jnp.float32), hbm
        scratch = [pltpu.VMEM(y.shape, jnp.float32), pltpu.SemaphoreType.DMA((2,))] + scratch
    else:
        shapes = (whole,) if k == DEG - 1 else (whole, rim, rim)
        specs = (vmem,) * len(shapes)
    return pl.pallas_call(
        functools.partial(step_kernel, first, final),
        out_shape=shapes,
        in_specs=[pl.BlockSpec(memory_space=pltpu.SMEM)] + [vmem] * len(args) + [hbm],
        out_specs=specs,
        scratch_shapes=scratch,
        compiler_params=pltpu.CompilerParams(vmem_limit_bytes=8 * 1024 * 1024),
        name="chebyshev_first" if first else "chebyshev_step",
    )(place, *args, token)


def blend(turn_ref, states_ref, part_ref, spot, p, row, count):
    panel = [part_ref[s, p, row, :] for s in range(count)]
    for t in range(count):
        total = states_ref[t, spot + p, row, :]
        for s in range(count):
            total = total + turn_ref[s, t] * panel[s]
        yield t, total


def rim_kernel(spots_ref, turn_ref, states_ref, *refs):
    parts, outs, rims_ref = refs[:4], refs[4:-1], refs[-1]
    count = states_ref.shape[0]
    width, rows = parts[0].shape[1:3]
    even = (spots_ref[12] & 1) == 0
    for k in range(4):
        spot, where = spots_ref[k], spots_ref[4 + k]

        def along(i, carry):
            row = pl.ds(pl.multiple_of(i * 8, 8), 8)
            for p in range(width):
                for t, total in blend(turn_ref, states_ref, parts[k], spot, p, row, count):
                    rims_ref[t, where + p, row, :] = total
            return carry

        lax.fori_loop(0, rows // 8, along, 0)

    for t in range(count):
        outs[2 * t][...] = rims_ref[t, :RIM]
        outs[2 * t + 1][...] = rims_ref[t, RIM:]


def body_kernel(spots_ref, turn_ref, states_ref, *refs):
    parts, rims, outs = refs[:4], refs[4:-2], refs[-2:]
    count, planes = states_ref.shape[:2]
    width, rows = parts[0].shape[1:3]
    for k in range(4):
        spot = spots_ref[8 + k]

        def along(i, carry):
            row = pl.ds(pl.multiple_of(i * 8, 8), 8)
            for p in range(width):
                for t, total in blend(turn_ref, states_ref, parts[k], spot, p, row, count):
                    outs[t][spot + p, row, :] = total
            return carry

        lax.fori_loop(0, rows // 8, along, 0)

    even = (spots_ref[12] & 1) == 0
    for t in range(count):
        near, far = rims[2 * t], rims[2 * t + 1]

        @pl.when(even)
        def _():
            outs[t][planes - RIM :] = near[...]
            outs[t][:RIM] = far[...]

        @pl.when(jnp.logical_not(even))
        def _():
            outs[t][:RIM] = near[...]
            outs[t][planes - RIM :] = far[...]


def mixed(kernel, name, spots, turn, states, args, shapes, scratch):
    vmem = pl.BlockSpec(memory_space=pltpu.VMEM)
    smem = pl.BlockSpec(memory_space=pltpu.SMEM)
    return pl.pallas_call(
        kernel,
        out_shape=[jax.ShapeDtypeStruct(s, jnp.float32) for s in shapes],
        in_specs=[smem, smem] + [vmem] * (1 + len(args)),
        out_specs=[vmem] * len(shapes),
        scratch_shapes=scratch,
        compiler_params=pltpu.CompilerParams(vmem_limit_bytes=8 * 1024 * 1024),
        name=name,
    )(spots, turn, states, *args)


def on_device(states, potential, rotation_panel, owner):
    size = lax.axis_size("dom")
    pairs = [(i, i ^ 1) for i in range(size)]
    others = [(i, (i + 1) % size if i % 2 else (i - 1) % size) for i in range(size)]
    depth = lax.axis_size("band") // 4
    count, planes, rows, lanes = states.shape

    def device(x, z, c):
        return (x * depth + z) * 2 + c

    chips = [(x, z, c) for x in range(2) for z in range(depth) for c in range(2)]
    swap_core = [(device(x, z, c), device(x, z, 1 - c)) for x, z, c in chips]
    swap_x = [(device(x, z, c), device(1 - x, z, c)) for x, z, c in chips]

    def shift(k):
        return [(device(x, z, c), device(x, (z + k) % depth, c)) for x, z, c in chips]

    mz_high, mz_low = halves(band_matrix(lanes, 1))
    my_high, my_low = halves(band_matrix(rows, GROUP))
    mz = jnp.asarray(np.concatenate([mz_high, mz_low, mz_high], axis=0))
    my = jnp.asarray(np.concatenate([my_high, my_high, my_low], axis=1))

    me = lax.axis_index("band")
    source = owner[0]
    away = me ^ source
    core_off = away & 1
    x_off = jnp.where(away >= 2 * depth, 1, 0)
    far_z = ((me >> 1) - (source >> 1)) & (depth - 1)
    slab = lax.axis_index("dom")
    place = jnp.stack([slab, jnp.int32(size - 1)])
    odd = slab & 1

    width = RIM // 2
    quarters = [(core_off ^ c) * 2 + (x_off ^ x) for c in (0, 1) for x in (0, 1)]
    rim_spots = [jnp.where(q >= 2, planes - RIM, 0) + width * (q & 1) for q in quarters]
    rim_slots = [RIM * (1 - ((q >> 1) ^ odd)) + width * (q & 1) for q in quarters]
    body_spots = [RIM + width * q for q in quarters]
    spots = jnp.stack(rim_spots + rim_slots + body_spots + [slab])

    def spread(keep, send, after):
        got = lax.ppermute(send, "band", swap_core)
        near = core_off == 0
        stay = jnp.where(near, keep[:, :width], got[:, :width])
        pass_on = jnp.where(near, keep[:, width:], got[:, width:])
        got = lax.ppermute(pass_on, "band", swap_x)
        here = jnp.where(x_off == 0, stay, got)
        if after is not None:
            here, _ = lax.optimization_barrier((here, after))
        up = lax.ppermute(here, "band", shift(1))
        down = lax.ppermute(here, "band", shift(-1))
        here = jnp.where(far_z == 1, up, jnp.where(far_z == depth - 1, down, here))
        step_one = here
        up = lax.ppermute(here, "band", shift(3))
        down = lax.ppermute(here, "band", shift(-3))
        rising = (far_z >= 2) & (far_z <= 4)
        falling = (far_z == 5) | (far_z == 6)
        here = jnp.where(rising, up, jnp.where(falling, down, here))
        there = lax.ppermute(here, "band", swap_x)
        return [
            here,
            there,
            lax.ppermute(here, "band", swap_core),
            lax.ppermute(there, "band", swap_core),
        ], step_one

    rim_parts, stage = spread(states[:, :RIM], states[:, planes - RIM :], None)
    middle = planes // 2
    body_parts, _ = spread(states[:, RIM:middle], states[:, middle : planes - RIM], None)
    rim_shape = (RIM, rows, lanes)
    rims = mixed(
        rim_kernel, "mix_rims", spots, rotation_panel, states, rim_parts,
        [rim_shape] * (2 * count), [pltpu.VMEM((count, 2 * RIM, rows, lanes), jnp.float32)],
    )
    edges = [(rims[2 * s], rims[2 * s + 1]) for s in range(count)]
    current = list(mixed(
        body_kernel, "mix_body", spots, rotation_panel, states, [*body_parts, *rims],
        [(planes, rows, lanes)] * count, [],
    ))
    previous = [None] * count
    token = potential
    for k in range(DEG):
        for s in range(count):
            one = lax.ppermute(edges[s][0], "dom", pairs)
            two = lax.ppermute(edges[s][1], "dom", others)
            final = k == DEG - 1 and s == count - 1
            out = step(
                k, final, place, current[s], one, two, previous[s], potential, mz, my, token
            )
            if final:
                return out
            previous[s], current[s] = current[s], out[0]
            token = out[1] if k < DEG - 1 else out[0]
            edges[s] = out[1:]


def solution(mesh):
    in_specs = (P("band", "dom", None, None), P("dom", None, None), P(None, "band"), P())
    out_specs = P("band", "dom", None, None)
    return jax.shard_map(
        on_device, mesh=mesh, in_specs=in_specs, out_specs=out_specs, check_vma=False
    )
```

```python
import functools

import jax
import jax.numpy as jnp
import ml_dtypes
import numpy as np
from jax import lax
from jax.experimental import pallas as pl
from jax.experimental.pallas import tpu as pltpu
from jax.sharding import PartitionSpec as P

DEG = 4
RIM = 6
WEIGHTS = (
    -5369.0 / 1800.0,
    12.0 / 7.0,
    -15.0 / 56.0,
    10.0 / 189.0,
    -1.0 / 112.0,
    2.0 / 1925.0,
    -1.0 / 16632.0,
)
CENTER = 8.0
HALF_WIDTH = 5.0
LAPLACE = -1.0 / HALF_WIDTH
SLOPE = 2.0 / HALF_WIDTH
SHIFT = -2.0 * CENTER / HALF_WIDTH + LAPLACE * 3.0 * WEIGHTS[0]
SPAN = [LAPLACE * w for w in WEIGHTS]
GROUP = 4


def band_matrix(size, copies):
    one = np.zeros((size, size), np.float64)
    for offset in range(1, RIM + 1):
        one += SPAN[offset] * (np.eye(size, k=offset) + np.eye(size, k=-offset))
    return np.kron(np.eye(copies), one).astype(np.float32)


def halves(matrix):
    high = matrix.astype(ml_dtypes.bfloat16)
    low = (matrix - high.astype(np.float32)).astype(ml_dtypes.bfloat16)
    return high, low


def second_differences(planes, y_ref, below_ref, above_ref, pot_ref, mz_ref, my_ref, prev_ref, next_ref):
    rows, lanes = y_ref.shape[1:]

    def along_plane(g, carry):
        group = pl.ds(pl.multiple_of(g * GROUP, GROUP), GROUP)
        block = y_ref[group].reshape(GROUP * rows, lanes)
        high = block.astype(jnp.bfloat16)
        low = (block - high.astype(jnp.float32)).astype(jnp.bfloat16)
        total = jnp.dot(
            jnp.concatenate([high, high, low], axis=1),
            mz_ref[...],
            preferred_element_type=jnp.float32,
        )
        total = total + jnp.dot(
            my_ref[...],
            jnp.concatenate([high, low, high], axis=0),
            preferred_element_type=jnp.float32,
        )
        next_ref[group] = total.reshape(GROUP, rows, lanes)
        return carry

    lax.fori_loop(0, planes // GROUP, along_plane, 0, unroll=2)

    def across_planes(i, carry):
        row = pl.ds(pl.multiple_of(i * 8, 8), 8)
        for j in range(lanes // 128):
            col = pl.ds(j * 128, 128)
            line = [below_ref[p, row, col] for p in range(RIM)]
            line += [y_ref[p, row, col] for p in range(planes)]
            line += [above_ref[p, row, col] for p in range(RIM)]
            for p in range(planes):
                here = p + RIM
                out = next_ref[p, row, col]
                for offset in range(1, RIM + 1):
                    out = out + SPAN[offset] * (line[here - offset] + line[here + offset])
                out = out + (SLOPE * pot_ref[p, row, col] + SHIFT) * line[here]
                if prev_ref is None:
                    next_ref[p, row, col] = 0.5 * out
                else:
                    next_ref[p, row, col] = out - prev_ref[p, row, col]
        return carry

    lax.fori_loop(0, rows // 8, across_planes, 0)


def step_kernel(first, final, place_ref, *refs):
    y_ref, odd_ref, even_ref = refs[:3]
    prev_ref = None if first else refs[3]
    refs = refs[3:] if first else refs[4:]
    pot_ref, mz_ref, my_ref, token_ref = refs[:4]
    below_ref, above_ref = refs[-2:]
    planes, rows, lanes = y_ref.shape
    place = place_ref[0]
    even = (place & 1) == 0
    last = place_ref[1]
    zero = jnp.zeros((rows, lanes), jnp.float32)
    for p in range(RIM):
        one, two = odd_ref[p], even_ref[p]
        below_ref[p] = jnp.where(place == 0, zero, jnp.where(even, two, one))
        above_ref[p] = jnp.where(place == last, zero, jnp.where(even, one, two))
    use = (y_ref, below_ref, above_ref, pot_ref, mz_ref, my_ref, prev_ref)

    if final:
        out_ref, next_ref, sems = refs[4:7]
        copies = [pltpu.make_async_copy(token_ref, out_ref.at[0], sems.at[0])]
        copies += [pltpu.make_async_copy(next_ref, out_ref.at[1], sems.at[1])]
        copies[0].start()
        second_differences(planes, *use, next_ref)
        copies[1].start()
        copies[0].wait()
        copies[1].wait()
        return

    next_ref = refs[4]
    second_differences(planes, *use, next_ref)
    if len(refs) == 7:
        return
    near_ref, far_ref = refs[5:7]

    @pl.when(even)
    def _():
        near_ref[...] = next_ref[planes - RIM :]
        far_ref[...] = next_ref[:RIM]

    @pl.when(jnp.logical_not(even))
    def _():
        near_ref[...] = next_ref[:RIM]
        far_ref[...] = next_ref[planes - RIM :]


def step(k, final, place, y, one, two, prev, potential, mz, my, token):
    first = k == 0
    args = [y, one, two] + ([] if first else [prev]) + [potential, mz, my]
    vmem = pl.BlockSpec(memory_space=pltpu.VMEM)
    hbm = pl.BlockSpec(memory_space=pl.ANY)
    rim = jax.ShapeDtypeStruct((RIM,) + y.shape[1:], jnp.float32)
    whole = jax.ShapeDtypeStruct(y.shape, jnp.float32)
    scratch = [pltpu.VMEM(rim.shape, jnp.float32)] * 2
    if final:
        shapes, specs = jax.ShapeDtypeStruct((2,) + y.shape, jnp.float32), hbm
        scratch = [pltpu.VMEM(y.shape, jnp.float32), pltpu.SemaphoreType.DMA((2,))] + scratch
    else:
        shapes = (whole,) if k == DEG - 1 else (whole, rim, rim)
        specs = (vmem,) * len(shapes)
    return pl.pallas_call(
        functools.partial(step_kernel, first, final),
        out_shape=shapes,
        in_specs=[pl.BlockSpec(memory_space=pltpu.SMEM)] + [vmem] * len(args) + [hbm],
        out_specs=specs,
        scratch_shapes=scratch,
        compiler_params=pltpu.CompilerParams(vmem_limit_bytes=8 * 1024 * 1024),
        name="chebyshev_first" if first else "chebyshev_step",
    )(place, *args, token)


def blend(turn_ref, states_ref, part_ref, spot, p, row, count):
    panel = [part_ref[s, p, row, :] for s in range(count)]
    for t in range(count):
        total = states_ref[t, spot + p, row, :]
        for s in range(count):
            total = total + turn_ref[s, t] * panel[s]
        yield t, total


def rim_kernel(spots_ref, turn_ref, states_ref, *refs):
    parts, outs, rims_ref = refs[:4], refs[4:-1], refs[-1]
    count = states_ref.shape[0]
    width, rows = parts[0].shape[1:3]
    even = (spots_ref[12] & 1) == 0
    for k in range(4):
        spot, where = spots_ref[k], spots_ref[4 + k]

        def along(i, carry):
            row = pl.ds(pl.multiple_of(i * 8, 8), 8)
            for p in range(width):
                for t, total in blend(turn_ref, states_ref, parts[k], spot, p, row, count):
                    rims_ref[t, where + p, row, :] = total
            return carry

        lax.fori_loop(0, rows // 8, along, 0)

    for t in range(count):
        outs[2 * t][...] = rims_ref[t, :RIM]
        outs[2 * t + 1][...] = rims_ref[t, RIM:]


def body_kernel(spots_ref, turn_ref, states_ref, *refs):
    parts, rims, outs = refs[:4], refs[4:-2], refs[-2:]
    count, planes = states_ref.shape[:2]
    width, rows = parts[0].shape[1:3]
    for k in range(4):
        spot = spots_ref[8 + k]

        def along(i, carry):
            row = pl.ds(pl.multiple_of(i * 8, 8), 8)
            for p in range(width):
                for t, total in blend(turn_ref, states_ref, parts[k], spot, p, row, count):
                    outs[t][spot + p, row, :] = total
            return carry

        lax.fori_loop(0, rows // 8, along, 0)

    even = (spots_ref[12] & 1) == 0
    for t in range(count):
        near, far = rims[2 * t], rims[2 * t + 1]

        @pl.when(even)
        def _():
            outs[t][planes - RIM :] = near[...]
            outs[t][:RIM] = far[...]

        @pl.when(jnp.logical_not(even))
        def _():
            outs[t][:RIM] = near[...]
            outs[t][planes - RIM :] = far[...]


def mixed(kernel, name, spots, turn, states, args, shapes, scratch):
    vmem = pl.BlockSpec(memory_space=pltpu.VMEM)
    smem = pl.BlockSpec(memory_space=pltpu.SMEM)
    return pl.pallas_call(
        kernel,
        out_shape=[jax.ShapeDtypeStruct(s, jnp.float32) for s in shapes],
        in_specs=[smem, smem] + [vmem] * (1 + len(args)),
        out_specs=[vmem] * len(shapes),
        scratch_shapes=scratch,
        compiler_params=pltpu.CompilerParams(vmem_limit_bytes=8 * 1024 * 1024),
        name=name,
    )(spots, turn, states, *args)


def on_device(states, potential, rotation_panel, owner):
    size = lax.axis_size("dom")
    pairs = [(i, i ^ 1) for i in range(size)]
    others = [(i, (i + 1) % size if i % 2 else (i - 1) % size) for i in range(size)]
    depth = lax.axis_size("band") // 4
    count, planes, rows, lanes = states.shape

    def device(x, z, c):
        return (x * depth + z) * 2 + c

    chips = [(x, z, c) for x in range(2) for z in range(depth) for c in range(2)]
    swap_core = [(device(x, z, c), device(x, z, 1 - c)) for x, z, c in chips]
    swap_x = [(device(x, z, c), device(1 - x, z, c)) for x, z, c in chips]

    def shift(k):
        return [(device(x, z, c), device(x, (z + k) % depth, c)) for x, z, c in chips]

    mz_high, mz_low = halves(band_matrix(lanes, 1))
    my_high, my_low = halves(band_matrix(rows, GROUP))
    mz = jnp.asarray(np.concatenate([mz_high, mz_low, mz_high], axis=0))
    my = jnp.asarray(np.concatenate([my_high, my_high, my_low], axis=1))

    me = lax.axis_index("band")
    source = owner[0]
    away = me ^ source
    core_off = away & 1
    x_off = jnp.where(away >= 2 * depth, 1, 0)
    far_z = ((me >> 1) - (source >> 1)) & (depth - 1)
    slab = lax.axis_index("dom")
    place = jnp.stack([slab, jnp.int32(size - 1)])
    odd = slab & 1

    width = RIM // 2
    quarters = [(core_off ^ c) * 2 + (x_off ^ x) for c in (0, 1) for x in (0, 1)]
    rim_spots = [jnp.where(q >= 2, planes - RIM, 0) + width * (q & 1) for q in quarters]
    rim_slots = [RIM * (1 - ((q >> 1) ^ odd)) + width * (q & 1) for q in quarters]
    body_spots = [RIM + width * q for q in quarters]
    spots = jnp.stack(rim_spots + rim_slots + body_spots + [slab])

    def gather(keep, send):
        got = lax.ppermute(send, "band", swap_core)
        near = core_off == 0
        stay = jnp.where(near, keep[:, :width], got[:, :width])
        pass_on = jnp.where(near, keep[:, width:], got[:, width:])
        got = lax.ppermute(pass_on, "band", swap_x)
        return [jnp.where(x_off == 0, stay[s], got[s]) for s in range(count)]

    middle = planes // 2
    chunks = gather(states[:, :RIM], states[:, planes - RIM :])
    chunks += gather(states[:, RIM:middle], states[:, middle : planes - RIM])
    rising = far_z <= depth // 2
    hops = jnp.where(rising, far_z, depth - far_z)
    stages = [chunks[0]]
    for stage in range(1, len(chunks) + depth // 2):
        up = lax.ppermute(stages[-1], "band", shift(1))
        down = lax.ppermute(stages[-1], "band", shift(-1))
        here = jnp.where(rising, up, down)
        if stage < len(chunks):
            here = jnp.where(hops == 0, chunks[stage], here)
        stages.append(here)

    def arrived(c):
        out = stages[c]
        for h in range(1, depth // 2 + 1):
            out = jnp.where(hops == h, stages[c + h], out)
        return out

    def share(unit):
        here = jnp.stack([arrived(unit * count + s) for s in range(count)])
        there = lax.ppermute(here, "band", swap_x)
        return [
            here,
            there,
            lax.ppermute(here, "band", swap_core),
            lax.ppermute(there, "band", swap_core),
        ]

    rim_parts, body_parts = share(0), share(1)
    rim_shape = (RIM, rows, lanes)
    rims = mixed(
        rim_kernel, "mix_rims", spots, rotation_panel, states, rim_parts,
        [rim_shape] * (2 * count), [pltpu.VMEM((count, 2 * RIM, rows, lanes), jnp.float32)],
    )
    edges = [(rims[2 * s], rims[2 * s + 1]) for s in range(count)]
    current = list(mixed(
        body_kernel, "mix_body", spots, rotation_panel, states, [*body_parts, *rims],
        [(planes, rows, lanes)] * count, [],
    ))
    previous = [None] * count
    token = potential
    for k in range(DEG):
        for s in range(count):
            one = lax.ppermute(edges[s][0], "dom", pairs)
            two = lax.ppermute(edges[s][1], "dom", others)
            if k == 0 and s == 0:
                edges[1], one, two = lax.optimization_barrier((edges[1], one, two))
            final = k == DEG - 1 and s == count - 1
            out = step(
                k, final, place, current[s], one, two, previous[s], potential, mz, my, token
            )
            if final:
                return out
            previous[s], current[s] = current[s], out[0]
            token = out[1] if k < DEG - 1 else out[0]
            edges[s] = out[1:]


def solution(mesh):
    in_specs = (P("band", "dom", None, None), P("dom", None, None), P(None, "band"), P())
    out_specs = P("band", "dom", None, None)
    return jax.shard_map(
        on_device, mesh=mesh, in_specs=in_specs, out_specs=out_specs, check_vma=False
    )
```

```python
import functools

import jax
import jax.numpy as jnp
import ml_dtypes
import numpy as np
from jax import lax
from jax.experimental import pallas as pl
from jax.experimental.pallas import tpu as pltpu
from jax.sharding import PartitionSpec as P

DEG = 4
RIM = 6
WEIGHTS = (
    -5369.0 / 1800.0,
    12.0 / 7.0,
    -15.0 / 56.0,
    10.0 / 189.0,
    -1.0 / 112.0,
    2.0 / 1925.0,
    -1.0 / 16632.0,
)
CENTER = 8.0
HALF_WIDTH = 5.0
LAPLACE = -1.0 / HALF_WIDTH
SLOPE = 2.0 / HALF_WIDTH
SHIFT = -2.0 * CENTER / HALF_WIDTH + LAPLACE * 3.0 * WEIGHTS[0]
SPAN = [LAPLACE * w for w in WEIGHTS]
GROUP = 4


def band_matrix(size, copies):
    one = np.zeros((size, size), np.float64)
    for offset in range(1, RIM + 1):
        one += SPAN[offset] * (np.eye(size, k=offset) + np.eye(size, k=-offset))
    return np.kron(np.eye(copies), one).astype(np.float32)


def halves(matrix):
    high = matrix.astype(ml_dtypes.bfloat16)
    low = (matrix - high.astype(np.float32)).astype(ml_dtypes.bfloat16)
    return high, low


def second_differences(planes, y_ref, below_ref, above_ref, pot_ref, mz_ref, my_ref, prev_ref, next_ref):
    rows, lanes = y_ref.shape[1:]

    def along_plane(g, carry):
        group = pl.ds(pl.multiple_of(g * GROUP, GROUP), GROUP)
        block = y_ref[group].reshape(GROUP * rows, lanes)
        high = block.astype(jnp.bfloat16)
        low = (block - high.astype(jnp.float32)).astype(jnp.bfloat16)
        total = jnp.dot(
            jnp.concatenate([high, high, low], axis=1),
            mz_ref[...],
            preferred_element_type=jnp.float32,
        )
        total = total + jnp.dot(
            my_ref[...],
            jnp.concatenate([high, low, high], axis=0),
            preferred_element_type=jnp.float32,
        )
        next_ref[group] = total.reshape(GROUP, rows, lanes)
        return carry

    lax.fori_loop(0, planes // GROUP, along_plane, 0, unroll=2)

    def across_planes(i, carry):
        row = pl.ds(pl.multiple_of(i * 8, 8), 8)
        for j in range(lanes // 128):
            col = pl.ds(j * 128, 128)
            line = [below_ref[p, row, col] for p in range(RIM)]
            line += [y_ref[p, row, col] for p in range(planes)]
            line += [above_ref[p, row, col] for p in range(RIM)]
            for p in range(planes):
                here = p + RIM
                out = next_ref[p, row, col]
                for offset in range(1, RIM + 1):
                    out = out + SPAN[offset] * (line[here - offset] + line[here + offset])
                out = out + (SLOPE * pot_ref[p, row, col] + SHIFT) * line[here]
                if prev_ref is None:
                    next_ref[p, row, col] = 0.5 * out
                else:
                    next_ref[p, row, col] = out - prev_ref[p, row, col]
        return carry

    lax.fori_loop(0, rows // 8, across_planes, 0)


def step_kernel(first, final, place_ref, *refs):
    y_ref, odd_ref, even_ref = refs[:3]
    prev_ref = None if first else refs[3]
    refs = refs[3:] if first else refs[4:]
    pot_ref, mz_ref, my_ref, token_ref = refs[:4]
    below_ref, above_ref = refs[-2:]
    planes, rows, lanes = y_ref.shape
    place = place_ref[0]
    even = (place & 1) == 0
    last = place_ref[1]
    zero = jnp.zeros((rows, lanes), jnp.float32)
    for p in range(RIM):
        one, two = odd_ref[p], even_ref[p]
        below_ref[p] = jnp.where(place == 0, zero, jnp.where(even, two, one))
        above_ref[p] = jnp.where(place == last, zero, jnp.where(even, one, two))
    use = (y_ref, below_ref, above_ref, pot_ref, mz_ref, my_ref, prev_ref)

    if final:
        out_ref, next_ref, sems = refs[4:7]
        copies = [pltpu.make_async_copy(token_ref, out_ref.at[0], sems.at[0])]
        copies += [pltpu.make_async_copy(next_ref, out_ref.at[1], sems.at[1])]
        copies[0].start()
        second_differences(planes, *use, next_ref)
        copies[1].start()
        copies[0].wait()
        copies[1].wait()
        return

    next_ref = refs[4]
    second_differences(planes, *use, next_ref)
    if len(refs) == 7:
        return
    near_ref, far_ref = refs[5:7]

    @pl.when(even)
    def _():
        near_ref[...] = next_ref[planes - RIM :]
        far_ref[...] = next_ref[:RIM]

    @pl.when(jnp.logical_not(even))
    def _():
        near_ref[...] = next_ref[:RIM]
        far_ref[...] = next_ref[planes - RIM :]


def step(k, final, place, y, one, two, prev, potential, mz, my, token):
    first = k == 0
    args = [y, one, two] + ([] if first else [prev]) + [potential, mz, my]
    vmem = pl.BlockSpec(memory_space=pltpu.VMEM)
    hbm = pl.BlockSpec(memory_space=pl.ANY)
    rim = jax.ShapeDtypeStruct((RIM,) + y.shape[1:], jnp.float32)
    whole = jax.ShapeDtypeStruct(y.shape, jnp.float32)
    scratch = [pltpu.VMEM(rim.shape, jnp.float32)] * 2
    if final:
        shapes, specs = jax.ShapeDtypeStruct((2,) + y.shape, jnp.float32), hbm
        scratch = [pltpu.VMEM(y.shape, jnp.float32), pltpu.SemaphoreType.DMA((2,))] + scratch
    else:
        shapes = (whole,) if k == DEG - 1 else (whole, rim, rim)
        specs = (vmem,) * len(shapes)
    return pl.pallas_call(
        functools.partial(step_kernel, first, final),
        out_shape=shapes,
        in_specs=[pl.BlockSpec(memory_space=pltpu.SMEM)] + [vmem] * len(args) + [hbm],
        out_specs=specs,
        scratch_shapes=scratch,
        compiler_params=pltpu.CompilerParams(vmem_limit_bytes=8 * 1024 * 1024),
        name="chebyshev_first" if first else "chebyshev_step",
    )(place, *args, token)


def blend(turn_ref, states_ref, part_ref, spot, p, row, count):
    panel = [part_ref[s, p, row, :] for s in range(count)]
    for t in range(count):
        total = states_ref[t, spot + p, row, :]
        for s in range(count):
            total = total + turn_ref[s, t] * panel[s]
        yield t, total


def rim_kernel(spots_ref, turn_ref, states_ref, *refs):
    parts, outs, rims_ref = refs[:4], refs[4:-1], refs[-1]
    count = states_ref.shape[0]
    width, rows = parts[0].shape[1:3]
    even = (spots_ref[12] & 1) == 0
    for k in range(4):
        spot, where = spots_ref[k], spots_ref[4 + k]

        def along(i, carry):
            row = pl.ds(pl.multiple_of(i * 8, 8), 8)
            for p in range(width):
                for t, total in blend(turn_ref, states_ref, parts[k], spot, p, row, count):
                    rims_ref[t, where + p, row, :] = total
            return carry

        lax.fori_loop(0, rows // 8, along, 0)

    for t in range(count):
        outs[2 * t][...] = rims_ref[t, :RIM]
        outs[2 * t + 1][...] = rims_ref[t, RIM:]


def body_kernel(spots_ref, turn_ref, states_ref, *refs):
    parts, rims, outs = refs[:4], refs[4:-2], refs[-2:]
    count, planes = states_ref.shape[:2]
    width, rows = parts[0].shape[1:3]
    for k in range(4):
        spot = spots_ref[8 + k]

        def along(i, carry):
            row = pl.ds(pl.multiple_of(i * 8, 8), 8)
            for p in range(width):
                for t, total in blend(turn_ref, states_ref, parts[k], spot, p, row, count):
                    outs[t][spot + p, row, :] = total
            return carry

        lax.fori_loop(0, rows // 8, along, 0)

    even = (spots_ref[12] & 1) == 0
    for t in range(count):
        near, far = rims[2 * t], rims[2 * t + 1]

        @pl.when(even)
        def _():
            outs[t][planes - RIM :] = near[...]
            outs[t][:RIM] = far[...]

        @pl.when(jnp.logical_not(even))
        def _():
            outs[t][:RIM] = near[...]
            outs[t][planes - RIM :] = far[...]


def mixed(kernel, name, spots, turn, states, args, shapes, scratch):
    vmem = pl.BlockSpec(memory_space=pltpu.VMEM)
    smem = pl.BlockSpec(memory_space=pltpu.SMEM)
    return pl.pallas_call(
        kernel,
        out_shape=[jax.ShapeDtypeStruct(s, jnp.float32) for s in shapes],
        in_specs=[smem, smem] + [vmem] * (1 + len(args)),
        out_specs=[vmem] * len(shapes),
        scratch_shapes=scratch,
        compiler_params=pltpu.CompilerParams(vmem_limit_bytes=8 * 1024 * 1024),
        name=name,
    )(spots, turn, states, *args)


def on_device(states, potential, rotation_panel, owner):
    size = lax.axis_size("dom")
    pairs = [(i, i ^ 1) for i in range(size)]
    others = [(i, (i + 1) % size if i % 2 else (i - 1) % size) for i in range(size)]
    depth = lax.axis_size("band") // 4
    count, planes, rows, lanes = states.shape

    def device(x, z, c):
        return (x * depth + z) * 2 + c

    chips = [(x, z, c) for x in range(2) for z in range(depth) for c in range(2)]
    swap_core = [(device(x, z, c), device(x, z, 1 - c)) for x, z, c in chips]
    swap_x = [(device(x, z, c), device(1 - x, z, c)) for x, z, c in chips]

    def shift(k):
        return [(device(x, z, c), device(x, (z + k) % depth, c)) for x, z, c in chips]

    mz_high, mz_low = halves(band_matrix(lanes, 1))
    my_high, my_low = halves(band_matrix(rows, GROUP))
    mz = jnp.asarray(np.concatenate([mz_high, mz_low, mz_high], axis=0))
    my = jnp.asarray(np.concatenate([my_high, my_high, my_low], axis=1))

    me = lax.axis_index("band")
    source = owner[0]
    away = me ^ source
    core_off = away & 1
    x_off = jnp.where(away >= 2 * depth, 1, 0)
    far_z = ((me >> 1) - (source >> 1)) & (depth - 1)
    slab = lax.axis_index("dom")
    place = jnp.stack([slab, jnp.int32(size - 1)])
    odd = slab & 1

    width = RIM // 2
    quarters = [(core_off ^ c) * 2 + (x_off ^ x) for c in (0, 1) for x in (0, 1)]
    rim_spots = [jnp.where(q >= 2, planes - RIM, 0) + width * (q & 1) for q in quarters]
    rim_slots = [RIM * (1 - ((q >> 1) ^ odd)) + width * (q & 1) for q in quarters]
    body_spots = [RIM + width * q for q in quarters]
    spots = jnp.stack(rim_spots + rim_slots + body_spots + [slab])

    def gather(keep, send):
        swapped = lax.ppermute(send, "band", swap_core)
        near = core_off == 0
        stay = jnp.where(near, keep[:, :width], swapped[:, :width])
        pass_on = jnp.where(near, keep[:, width:], swapped[:, width:])
        got = lax.ppermute(pass_on, "band", swap_x)
        return jnp.where(x_off == 0, stay, got), swapped

    middle = planes // 2
    chunk, swapped = gather(states[:, :RIM], states[:, planes - RIM :])
    later, _ = lax.optimization_barrier((states, swapped))
    chunks = [chunk, gather(later[:, RIM:middle], later[:, middle : planes - RIM])[0]]
    rising = far_z <= depth // 2
    hops = jnp.where(rising, far_z, depth - far_z)

    def arrived(c):
        out = stages[c]
        for h in range(1, depth // 2 + 1):
            out = jnp.where(hops == h, stages[c + h], out)
        return out

    def share(here, there):
        return [
            here,
            there,
            lax.ppermute(here, "band", swap_core),
            lax.ppermute(there, "band", swap_core),
        ]

    stages = [chunks[0]]
    for stage in range(1, len(chunks) + depth // 2):
        sent = stages[-1]
        up = lax.ppermute(sent, "band", shift(1))
        down = lax.ppermute(sent, "band", shift(-1))
        here = jnp.where(rising, up, down)
        if stage < len(chunks):
            here = jnp.where(hops == 0, chunks[stage], here)
        stages.append(here)

    here = arrived(0)
    rim_parts = share(here, lax.ppermute(here, "band", swap_x))
    rim_shape = (RIM, rows, lanes)
    rims = mixed(
        rim_kernel, "mix_rims", spots, rotation_panel, states, rim_parts,
        [rim_shape] * (2 * count), [pltpu.VMEM((count, 2 * RIM, rows, lanes), jnp.float32)],
    )
    edges = [(rims[2 * s], rims[2 * s + 1]) for s in range(count)]
    here = arrived(1)

    body_parts = share(here, lax.ppermute(here, "band", swap_x))
    current = list(mixed(
        body_kernel, "mix_body", spots, rotation_panel, states, [*body_parts, *rims],
        [(planes, rows, lanes)] * count, [],
    ))
    previous = [None] * count
    token = potential
    for k in range(DEG):
        for s in range(count):
            one = lax.ppermute(edges[s][0], "dom", pairs)
            two = lax.ppermute(edges[s][1], "dom", others)
            if k == 0 and s == 0:
                edges[1], one, two = lax.optimization_barrier((edges[1], one, two))
            final = k == DEG - 1 and s == count - 1
            out = step(
                k, final, place, current[s], one, two, previous[s], potential, mz, my, token
            )
            if final:
                return out
            previous[s], current[s] = current[s], out[0]
            token = out[1] if k < DEG - 1 else out[0]
            edges[s] = out[1:]


def solution(mesh):
    in_specs = (P("band", "dom", None, None), P("dom", None, None), P(None, "band"), P())
    out_specs = P("band", "dom", None, None)
    return jax.shard_map(
        on_device, mesh=mesh, in_specs=in_specs, out_specs=out_specs, check_vma=False
    )
```

```python
import functools

import jax
import jax.numpy as jnp
import ml_dtypes
import numpy as np
from jax import lax
from jax.experimental import pallas as pl
from jax.experimental.pallas import tpu as pltpu
from jax.sharding import PartitionSpec as P

DEG = 4
RIM = 6
WEIGHTS = (
    -5369.0 / 1800.0,
    12.0 / 7.0,
    -15.0 / 56.0,
    10.0 / 189.0,
    -1.0 / 112.0,
    2.0 / 1925.0,
    -1.0 / 16632.0,
)
CENTER = 8.0
HALF_WIDTH = 5.0
LAPLACE = -1.0 / HALF_WIDTH
SLOPE = 2.0 / HALF_WIDTH
SHIFT = -2.0 * CENTER / HALF_WIDTH + LAPLACE * 3.0 * WEIGHTS[0]
SPAN = [LAPLACE * w for w in WEIGHTS]
GROUP = 4


def band_matrix(size, copies):
    one = np.zeros((size, size), np.float64)
    for offset in range(1, RIM + 1):
        one += SPAN[offset] * (np.eye(size, k=offset) + np.eye(size, k=-offset))
    return np.kron(np.eye(copies), one).astype(np.float32)


def halves(matrix):
    high = matrix.astype(ml_dtypes.bfloat16)
    low = (matrix - high.astype(np.float32)).astype(ml_dtypes.bfloat16)
    return high, low


def second_differences(planes, y_ref, below_ref, above_ref, pot_ref, mz_ref, my_ref, prev_ref, next_ref):
    rows, lanes = y_ref.shape[1:]

    def along_plane(g, carry):
        group = pl.ds(pl.multiple_of(g * GROUP, GROUP), GROUP)
        block = y_ref[group].reshape(GROUP * rows, lanes)
        high = block.astype(jnp.bfloat16)
        low = (block - high.astype(jnp.float32)).astype(jnp.bfloat16)
        total = jnp.dot(
            jnp.concatenate([high, high, low], axis=1),
            mz_ref[...],
            preferred_element_type=jnp.float32,
        )
        total = total + jnp.dot(
            my_ref[...],
            jnp.concatenate([high, low, high], axis=0),
            preferred_element_type=jnp.float32,
        )
        next_ref[group] = total.reshape(GROUP, rows, lanes)
        return carry

    lax.fori_loop(0, planes // GROUP, along_plane, 0, unroll=2)

    def across_planes(i, carry):
        row = pl.ds(pl.multiple_of(i * 8, 8), 8)
        for j in range(lanes // 128):
            col = pl.ds(j * 128, 128)
            line = [below_ref[p, row, col] for p in range(RIM)]
            line += [y_ref[p, row, col] for p in range(planes)]
            line += [above_ref[p, row, col] for p in range(RIM)]
            for p in range(planes):
                here = p + RIM
                out = next_ref[p, row, col]
                for offset in range(1, RIM + 1):
                    out = out + SPAN[offset] * (line[here - offset] + line[here + offset])
                out = out + (SLOPE * pot_ref[p, row, col] + SHIFT) * line[here]
                if prev_ref is None:
                    next_ref[p, row, col] = 0.5 * out
                else:
                    next_ref[p, row, col] = out - prev_ref[p, row, col]
        return carry

    lax.fori_loop(0, rows // 8, across_planes, 0)


def step_kernel(first, final, place_ref, *refs):
    y_ref, odd_ref, even_ref = refs[:3]
    prev_ref = None if first else refs[3]
    refs = refs[3:] if first else refs[4:]
    pot_ref, mz_ref, my_ref, token_ref = refs[:4]
    below_ref, above_ref = refs[-2:]
    planes, rows, lanes = y_ref.shape
    place = place_ref[0]
    even = (place & 1) == 0
    last = place_ref[1]
    zero = jnp.zeros((rows, lanes), jnp.float32)
    for p in range(RIM):
        one, two = odd_ref[p], even_ref[p]
        below_ref[p] = jnp.where(place == 0, zero, jnp.where(even, two, one))
        above_ref[p] = jnp.where(place == last, zero, jnp.where(even, one, two))
    use = (y_ref, below_ref, above_ref, pot_ref, mz_ref, my_ref, prev_ref)

    if final:
        out_ref, next_ref, sems = refs[4:7]
        copies = [pltpu.make_async_copy(token_ref, out_ref.at[0], sems.at[0])]
        copies += [pltpu.make_async_copy(next_ref, out_ref.at[1], sems.at[1])]
        copies[0].start()
        second_differences(planes, *use, next_ref)
        copies[1].start()
        copies[0].wait()
        copies[1].wait()
        return

    next_ref = refs[4]
    second_differences(planes, *use, next_ref)
    if len(refs) == 7:
        return
    near_ref, far_ref = refs[5:7]

    @pl.when(even)
    def _():
        near_ref[...] = next_ref[planes - RIM :]
        far_ref[...] = next_ref[:RIM]

    @pl.when(jnp.logical_not(even))
    def _():
        near_ref[...] = next_ref[:RIM]
        far_ref[...] = next_ref[planes - RIM :]


def step(k, final, place, y, one, two, prev, potential, mz, my, token):
    first = k == 0
    args = [y, one, two] + ([] if first else [prev]) + [potential, mz, my]
    vmem = pl.BlockSpec(memory_space=pltpu.VMEM)
    hbm = pl.BlockSpec(memory_space=pl.ANY)
    rim = jax.ShapeDtypeStruct((RIM,) + y.shape[1:], jnp.float32)
    whole = jax.ShapeDtypeStruct(y.shape, jnp.float32)
    scratch = [pltpu.VMEM(rim.shape, jnp.float32)] * 2
    if final:
        shapes, specs = jax.ShapeDtypeStruct((2,) + y.shape, jnp.float32), hbm
        scratch = [pltpu.VMEM(y.shape, jnp.float32), pltpu.SemaphoreType.DMA((2,))] + scratch
    else:
        shapes = (whole,) if k == DEG - 1 else (whole, rim, rim)
        specs = (vmem,) * len(shapes)
    return pl.pallas_call(
        functools.partial(step_kernel, first, final),
        out_shape=shapes,
        in_specs=[pl.BlockSpec(memory_space=pltpu.SMEM)] + [vmem] * len(args) + [hbm],
        out_specs=specs,
        scratch_shapes=scratch,
        compiler_params=pltpu.CompilerParams(vmem_limit_bytes=8 * 1024 * 1024),
        name="chebyshev_first" if first else "chebyshev_step",
    )(place, *args, token)


def blend(turn_ref, states_ref, part_ref, spot, p, row, count):
    panel = [part_ref[s, p, row, :] for s in range(count)]
    for t in range(count):
        total = states_ref[t, spot + p, row, :]
        for s in range(count):
            total = total + turn_ref[s, t] * panel[s]
        yield t, total


def rim_kernel(spots_ref, turn_ref, states_ref, *refs):
    parts, outs, rims_ref = refs[:4], refs[4:-1], refs[-1]
    count = states_ref.shape[0]
    width, rows = parts[0].shape[1:3]
    even = (spots_ref[12] & 1) == 0
    for k in range(4):
        spot, where = spots_ref[k], spots_ref[4 + k]

        def along(i, carry):
            row = pl.ds(pl.multiple_of(i * 8, 8), 8)
            for p in range(width):
                for t, total in blend(turn_ref, states_ref, parts[k], spot, p, row, count):
                    rims_ref[t, where + p, row, :] = total
            return carry

        lax.fori_loop(0, rows // 8, along, 0)

    for t in range(count):
        outs[2 * t][...] = rims_ref[t, :RIM]
        outs[2 * t + 1][...] = rims_ref[t, RIM:]


def body_kernel(spots_ref, turn_ref, states_ref, *refs):
    parts, rims, outs = refs[:4], refs[4:-2], refs[-2:]
    count, planes = states_ref.shape[:2]
    width, rows = parts[0].shape[1:3]
    for k in range(4):
        spot = spots_ref[8 + k]

        def along(i, carry):
            row = pl.ds(pl.multiple_of(i * 8, 8), 8)
            for p in range(width):
                for t, total in blend(turn_ref, states_ref, parts[k], spot, p, row, count):
                    outs[t][spot + p, row, :] = total
            return carry

        lax.fori_loop(0, rows // 8, along, 0)

    even = (spots_ref[12] & 1) == 0
    for t in range(count):
        near, far = rims[2 * t], rims[2 * t + 1]

        @pl.when(even)
        def _():
            outs[t][planes - RIM :] = near[...]
            outs[t][:RIM] = far[...]

        @pl.when(jnp.logical_not(even))
        def _():
            outs[t][:RIM] = near[...]
            outs[t][planes - RIM :] = far[...]


def mixed(kernel, name, spots, turn, states, args, shapes, scratch):
    vmem = pl.BlockSpec(memory_space=pltpu.VMEM)
    smem = pl.BlockSpec(memory_space=pltpu.SMEM)
    return pl.pallas_call(
        kernel,
        out_shape=[jax.ShapeDtypeStruct(s, jnp.float32) for s in shapes],
        in_specs=[smem, smem] + [vmem] * (1 + len(args)),
        out_specs=[vmem] * len(shapes),
        scratch_shapes=scratch,
        compiler_params=pltpu.CompilerParams(vmem_limit_bytes=8 * 1024 * 1024),
        name=name,
    )(spots, turn, states, *args)


def on_device(states, potential, rotation_panel, owner):
    size = lax.axis_size("dom")
    pairs = [(i, i ^ 1) for i in range(size)]
    ends = (0, size - 1)
    others = [(i, i if i in ends else i + 1 if i % 2 else i - 1) for i in range(size)]
    depth = lax.axis_size("band") // 4
    count, planes, rows, lanes = states.shape

    def device(x, z, c):
        return (x * depth + z) * 2 + c

    chips = [(x, z, c) for x in range(2) for z in range(depth) for c in range(2)]
    swap_core = [(device(x, z, c), device(x, z, 1 - c)) for x, z, c in chips]
    swap_x = [(device(x, z, c), device(1 - x, z, c)) for x, z, c in chips]

    def shift(k):
        return [(device(x, z, c), device(x, (z + k) % depth, c)) for x, z, c in chips]

    mz_high, mz_low = halves(band_matrix(lanes, 1))
    my_high, my_low = halves(band_matrix(rows, GROUP))
    mz = jnp.asarray(np.concatenate([mz_high, mz_low, mz_high], axis=0))
    my = jnp.asarray(np.concatenate([my_high, my_high, my_low], axis=1))

    me = lax.axis_index("band")
    source = owner[0]
    away = me ^ source
    core_off = away & 1
    x_off = jnp.where(away >= 2 * depth, 1, 0)
    far_z = ((me >> 1) - (source >> 1)) & (depth - 1)
    slab = lax.axis_index("dom")
    place = jnp.stack([slab, jnp.int32(size - 1)])
    odd = slab & 1

    width = RIM // 2
    quarters = [(core_off ^ c) * 2 + (x_off ^ x) for c in (0, 1) for x in (0, 1)]
    rim_spots = [jnp.where(q >= 2, planes - RIM, 0) + width * (q & 1) for q in quarters]
    rim_slots = [RIM * (1 - ((q >> 1) ^ odd)) + width * (q & 1) for q in quarters]
    body_spots = [RIM + width * q for q in quarters]
    spots = jnp.stack(rim_spots + rim_slots + body_spots + [slab])

    def gather(keep, send):
        swapped = lax.ppermute(send, "band", swap_core)
        near = core_off == 0
        stay = jnp.where(near, keep[:, :width], swapped[:, :width])
        pass_on = jnp.where(near, keep[:, width:], swapped[:, width:])
        got = lax.ppermute(pass_on, "band", swap_x)
        return jnp.where(x_off == 0, stay, got), swapped

    middle = planes // 2
    chunk, swapped = gather(states[:, :RIM], states[:, planes - RIM :])
    later, _ = lax.optimization_barrier((states, swapped))
    chunks = [chunk, gather(later[:, RIM:middle], later[:, middle : planes - RIM])[0]]
    rising = far_z <= depth // 2
    hops = jnp.where(rising, far_z, depth - far_z)

    def arrived(c):
        out = stages[c]
        for h in range(1, depth // 2 + 1):
            out = jnp.where(hops == h, stages[c + h], out)
        return out

    def share(here, there):
        return [
            here,
            there,
            lax.ppermute(here, "band", swap_core),
            lax.ppermute(there, "band", swap_core),
        ]

    stages = [chunks[0]]
    for stage in range(1, len(chunks) + depth // 2):
        sent = stages[-1]
        up = lax.ppermute(sent, "band", shift(1))
        down = lax.ppermute(sent, "band", shift(-1))
        here = jnp.where(rising, up, down)
        if stage < len(chunks):
            here = jnp.where(hops == 0, chunks[stage], here)
        stages.append(here)

    here = arrived(0)
    rim_parts = share(here, lax.ppermute(here, "band", swap_x))
    rim_shape = (RIM, rows, lanes)
    rims = mixed(
        rim_kernel, "mix_rims", spots, rotation_panel, states, rim_parts,
        [rim_shape] * (2 * count), [pltpu.VMEM((count, 2 * RIM, rows, lanes), jnp.float32)],
    )
    edges = [(rims[2 * s], rims[2 * s + 1]) for s in range(count)]
    here = arrived(1)
    body_parts = share(here, lax.ppermute(here, "band", swap_x))
    current = list(mixed(
        body_kernel, "mix_body", spots, rotation_panel, states, [*body_parts, *rims],
        [(planes, rows, lanes)] * count, [],
    ))
    previous = [None] * count
    token = potential
    for k in range(DEG):
        for s in range(count):
            one = lax.ppermute(edges[s][0], "dom", pairs)
            two = lax.ppermute(edges[s][1], "dom", others)
            if k == 0 and s == 0:
                edges[1], one, two = lax.optimization_barrier((edges[1], one, two))
            final = k == DEG - 1 and s == count - 1
            out = step(
                k, final, place, current[s], one, two, previous[s], potential, mz, my, token
            )
            if final:
                return out
            previous[s], current[s] = current[s], out[0]
            token = out[1] if k < DEG - 1 else out[0]
            edges[s] = out[1:]


def solution(mesh):
    in_specs = (P("band", "dom", None, None), P("dom", None, None), P(None, "band"), P())
    out_specs = P("band", "dom", None, None)
    return jax.shard_map(
        on_device, mesh=mesh, in_specs=in_specs, out_specs=out_specs, check_vma=False
    )
```

```python
import functools

import jax
import jax.numpy as jnp
import ml_dtypes
import numpy as np
from jax import lax
from jax.experimental import pallas as pl
from jax.experimental.pallas import tpu as pltpu
from jax.sharding import PartitionSpec as P

DEG = 4
RIM = 6
WEIGHTS = (
    -5369.0 / 1800.0,
    12.0 / 7.0,
    -15.0 / 56.0,
    10.0 / 189.0,
    -1.0 / 112.0,
    2.0 / 1925.0,
    -1.0 / 16632.0,
)
CENTER = 8.0
HALF_WIDTH = 5.0
LAPLACE = -1.0 / HALF_WIDTH
SLOPE = 2.0 / HALF_WIDTH
SHIFT = -2.0 * CENTER / HALF_WIDTH + LAPLACE * 3.0 * WEIGHTS[0]
SPAN = [LAPLACE * w for w in WEIGHTS]
GROUP = 4


def band_matrix(size, copies):
    one = np.zeros((size, size), np.float64)
    for offset in range(1, RIM + 1):
        one += SPAN[offset] * (np.eye(size, k=offset) + np.eye(size, k=-offset))
    return np.kron(np.eye(copies), one).astype(np.float32)


def halves(matrix):
    high = matrix.astype(ml_dtypes.bfloat16)
    low = (matrix - high.astype(np.float32)).astype(ml_dtypes.bfloat16)
    return high, low


def second_differences(planes, y_ref, below_ref, above_ref, pot_ref, mz_ref, my_ref, prev_ref, next_ref):
    rows, lanes = y_ref.shape[1:]

    def along_plane(g, carry):
        group = pl.ds(pl.multiple_of(g * GROUP, GROUP), GROUP)
        block = y_ref[group].reshape(GROUP * rows, lanes)
        high = block.astype(jnp.bfloat16)
        low = (block - high.astype(jnp.float32)).astype(jnp.bfloat16)
        total = jnp.dot(
            jnp.concatenate([high, high, low], axis=1),
            mz_ref[...],
            preferred_element_type=jnp.float32,
        )
        total = total + jnp.dot(
            my_ref[...],
            jnp.concatenate([high, low, high], axis=0),
            preferred_element_type=jnp.float32,
        )
        next_ref[group] = total.reshape(GROUP, rows, lanes)
        return carry

    lax.fori_loop(0, planes // GROUP, along_plane, 0, unroll=2)

    def across_planes(i, carry):
        row = pl.ds(pl.multiple_of(i * 8, 8), 8)
        for j in range(lanes // 128):
            col = pl.ds(j * 128, 128)
            line = [below_ref[p, row, col] for p in range(RIM)]
            line += [y_ref[p, row, col] for p in range(planes)]
            line += [above_ref[p, row, col] for p in range(RIM)]
            for p in range(planes):
                here = p + RIM
                out = next_ref[p, row, col]
                for offset in range(1, RIM + 1):
                    out = out + SPAN[offset] * (line[here - offset] + line[here + offset])
                out = out + (SLOPE * pot_ref[p, row, col] + SHIFT) * line[here]
                if prev_ref is None:
                    next_ref[p, row, col] = 0.5 * out
                else:
                    next_ref[p, row, col] = out - prev_ref[p, row, col]
        return carry

    lax.fori_loop(0, rows // 8, across_planes, 0)


def step_kernel(first, final, place_ref, *refs):
    y_ref, odd_ref, even_ref = refs[:3]
    prev_ref = None if first else refs[3]
    refs = refs[3:] if first else refs[4:]
    pot_ref, mz_ref, my_ref, token_ref = refs[:4]
    below_ref, above_ref = refs[-2:]
    planes, rows, lanes = y_ref.shape
    place = place_ref[0]
    even = (place & 1) == 0
    last = place_ref[1]
    zero = jnp.zeros((rows, lanes), jnp.float32)
    for p in range(RIM):
        one, two = odd_ref[p], even_ref[p]
        below_ref[p] = jnp.where(place == 0, zero, jnp.where(even, two, one))
        above_ref[p] = jnp.where(place == last, zero, jnp.where(even, one, two))
    use = (y_ref, below_ref, above_ref, pot_ref, mz_ref, my_ref, prev_ref)

    if final:
        out_ref, next_ref, sems = refs[4:7]
        copies = [pltpu.make_async_copy(token_ref, out_ref.at[0], sems.at[0])]
        copies += [pltpu.make_async_copy(next_ref, out_ref.at[1], sems.at[1])]
        copies[0].start()
        second_differences(planes, *use, next_ref)
        copies[1].start()
        copies[0].wait()
        copies[1].wait()
        return

    next_ref = refs[4]
    second_differences(planes, *use, next_ref)
    if len(refs) == 7:
        return
    near_ref, far_ref = refs[5:7]

    @pl.when(even)
    def _():
        near_ref[...] = next_ref[planes - RIM :]
        far_ref[...] = next_ref[:RIM]

    @pl.when(jnp.logical_not(even))
    def _():
        near_ref[...] = next_ref[:RIM]
        far_ref[...] = next_ref[planes - RIM :]


def step(k, final, place, y, one, two, prev, potential, mz, my, token):
    first = k == 0
    args = [y, one, two] + ([] if first else [prev]) + [potential, mz, my]
    vmem = pl.BlockSpec(memory_space=pltpu.VMEM)
    hbm = pl.BlockSpec(memory_space=pl.ANY)
    rim = jax.ShapeDtypeStruct((RIM,) + y.shape[1:], jnp.float32)
    whole = jax.ShapeDtypeStruct(y.shape, jnp.float32)
    scratch = [pltpu.VMEM(rim.shape, jnp.float32)] * 2
    if final:
        shapes, specs = jax.ShapeDtypeStruct((2,) + y.shape, jnp.float32), hbm
        scratch = [pltpu.VMEM(y.shape, jnp.float32), pltpu.SemaphoreType.DMA((2,))] + scratch
    else:
        shapes = (whole,) if k == DEG - 1 else (whole, rim, rim)
        specs = (vmem,) * len(shapes)
    return pl.pallas_call(
        functools.partial(step_kernel, first, final),
        out_shape=shapes,
        in_specs=[pl.BlockSpec(memory_space=pltpu.SMEM)] + [vmem] * len(args) + [hbm],
        out_specs=specs,
        scratch_shapes=scratch,
        compiler_params=pltpu.CompilerParams(vmem_limit_bytes=8 * 1024 * 1024),
        name="chebyshev_first" if first else "chebyshev_step",
    )(place, *args, token)


def blend(turn_ref, states_ref, part_ref, spot, p, row, count):
    panel = [part_ref[s, p, row, :] for s in range(count)]
    for t in range(count):
        total = states_ref[t, spot + p, row, :]
        for s in range(count):
            total = total + turn_ref[s, t] * panel[s]
        yield t, total


def rim_kernel(spots_ref, turn_ref, states_ref, *refs):
    parts, outs, rims_ref = refs[:4], refs[4:-1], refs[-1]
    count = states_ref.shape[0]
    width, rows = parts[0].shape[1:3]
    even = (spots_ref[12] & 1) == 0
    for k in range(4):
        spot, where = spots_ref[k], spots_ref[4 + k]

        def along(i, carry):
            row = pl.ds(pl.multiple_of(i * 8, 8), 8)
            for p in range(width):
                for t, total in blend(turn_ref, states_ref, parts[k], spot, p, row, count):
                    rims_ref[t, where + p, row, :] = total
            return carry

        lax.fori_loop(0, rows // 8, along, 0)

    for t in range(count):
        outs[2 * t][...] = rims_ref[t, :RIM]
        outs[2 * t + 1][...] = rims_ref[t, RIM:]


def body_kernel(spots_ref, turn_ref, states_ref, *refs):
    parts, rims, outs = refs[:4], refs[4:-2], refs[-2:]
    count, planes = states_ref.shape[:2]
    width, rows = parts[0].shape[1:3]
    for k in range(4):
        spot = spots_ref[8 + k]

        def along(i, carry):
            row = pl.ds(pl.multiple_of(i * 8, 8), 8)
            for p in range(width):
                for t, total in blend(turn_ref, states_ref, parts[k], spot, p, row, count):
                    outs[t][spot + p, row, :] = total
            return carry

        lax.fori_loop(0, rows // 8, along, 0)

    even = (spots_ref[12] & 1) == 0
    for t in range(count):
        near, far = rims[2 * t], rims[2 * t + 1]

        @pl.when(even)
        def _():
            outs[t][planes - RIM :] = near[...]
            outs[t][:RIM] = far[...]

        @pl.when(jnp.logical_not(even))
        def _():
            outs[t][:RIM] = near[...]
            outs[t][planes - RIM :] = far[...]


def mixed(kernel, name, spots, turn, states, args, shapes, scratch):
    vmem = pl.BlockSpec(memory_space=pltpu.VMEM)
    smem = pl.BlockSpec(memory_space=pltpu.SMEM)
    return pl.pallas_call(
        kernel,
        out_shape=[jax.ShapeDtypeStruct(s, jnp.float32) for s in shapes],
        in_specs=[smem, smem] + [vmem] * (1 + len(args)),
        out_specs=[vmem] * len(shapes),
        scratch_shapes=scratch,
        compiler_params=pltpu.CompilerParams(vmem_limit_bytes=8 * 1024 * 1024),
        name=name,
    )(spots, turn, states, *args)


def on_device(states, potential, rotation_panel, owner):
    size = lax.axis_size("dom")
    pairs = [(i, i ^ 1) for i in range(size)]
    others = [(i, (i + 1) % size if i % 2 else (i - 1) % size) for i in range(size)]
    depth = lax.axis_size("band") // 4
    count, planes, rows, lanes = states.shape

    def device(x, z, c):
        return (x * depth + z) * 2 + c

    chips = [(x, z, c) for x in range(2) for z in range(depth) for c in range(2)]
    swap_core = [(device(x, z, c), device(x, z, 1 - c)) for x, z, c in chips]
    swap_x = [(device(x, z, c), device(1 - x, z, c)) for x, z, c in chips]

    def shift(k):
        return [(device(x, z, c), device(x, (z + k) % depth, c)) for x, z, c in chips]

    mz_high, mz_low = halves(band_matrix(lanes, 1))
    my_high, my_low = halves(band_matrix(rows, GROUP))
    mz = jnp.asarray(np.concatenate([mz_high, mz_low, mz_high], axis=0))
    my = jnp.asarray(np.concatenate([my_high, my_high, my_low], axis=1))

    me = lax.axis_index("band")
    source = owner[0]
    away = me ^ source
    core_off = away & 1
    x_off = jnp.where(away >= 2 * depth, 1, 0)
    far_z = ((me >> 1) - (source >> 1)) & (depth - 1)
    slab = lax.axis_index("dom")
    place = jnp.stack([slab, jnp.int32(size - 1)])
    odd = slab & 1

    width = RIM // 2
    quarters = [(core_off ^ c) * 2 + (x_off ^ x) for c in (0, 1) for x in (0, 1)]
    rim_spots = [jnp.where(q >= 2, planes - RIM, 0) + width * (q & 1) for q in quarters]
    rim_slots = [RIM * (1 - ((q >> 1) ^ odd)) + width * (q & 1) for q in quarters]
    body_spots = [RIM + width * q for q in quarters]
    spots = jnp.stack(rim_spots + rim_slots + body_spots + [slab])

    middle = planes // 2
    got = lax.ppermute(states[:, middle:], "band", swap_core)
    near = core_off == 0
    cuts = [(0, middle - RIM), (RIM, 0)]
    stay = [jnp.where(near, states[:, i : i + width], got[:, j : j + width]) for i, j in cuts]
    pass_on = jnp.stack(
        [
            jnp.where(near, states[:, i + width : i + RIM], got[:, j + width : j + RIM])
            for i, j in cuts
        ]
    )
    got = lax.ppermute(pass_on, "band", swap_x)
    chunks = [jnp.where(x_off == 0, stay[u], got[u]) for u in range(2)]
    rising = far_z <= depth // 2
    hops = jnp.where(rising, far_z, depth - far_z)

    def arrived(c):
        out = stages[c]
        for h in range(1, depth // 2 + 1):
            out = jnp.where(hops == h, stages[c + h], out)
        return out

    def share(here, there):
        return [
            here,
            there,
            lax.ppermute(here, "band", swap_core),
            lax.ppermute(there, "band", swap_core),
        ]

    stages = [chunks[0]]
    for stage in range(1, len(chunks) + depth // 2):
        sent = stages[-1]
        up = lax.ppermute(sent, "band", shift(1))
        down = lax.ppermute(sent, "band", shift(-1))
        here = jnp.where(rising, up, down)
        if stage < len(chunks):
            here = jnp.where(hops == 0, chunks[stage], here)
        stages.append(here)

    here = arrived(0)
    rim_parts = share(here, lax.ppermute(here, "band", swap_x))
    rim_shape = (RIM, rows, lanes)
    rims = mixed(
        rim_kernel, "mix_rims", spots, rotation_panel, states, rim_parts,
        [rim_shape] * (2 * count), [pltpu.VMEM((count, 2 * RIM, rows, lanes), jnp.float32)],
    )
    edges = [(rims[2 * s], rims[2 * s + 1]) for s in range(count)]
    here = arrived(1)
    body_parts = share(here, lax.ppermute(here, "band", swap_x))
    current = list(mixed(
        body_kernel, "mix_body", spots, rotation_panel, states, [*body_parts, *rims],
        [(planes, rows, lanes)] * count, [],
    ))
    previous = [None] * count
    token = potential
    for k in range(DEG):
        for s in range(count):
            one = lax.ppermute(edges[s][0], "dom", pairs)
            two = lax.ppermute(edges[s][1], "dom", others)
            if k == 0 and s == 0:
                edges[1], one, two, *current = lax.optimization_barrier((edges[1], one, two, *current))
            final = k == DEG - 1 and s == count - 1
            out = step(
                k, final, place, current[s], one, two, previous[s], potential, mz, my, token
            )
            if final:
                return out
            previous[s], current[s] = current[s], out[0]
            token = out[1] if k < DEG - 1 else out[0]
            edges[s] = out[1:]


def solution(mesh):
    in_specs = (P("band", "dom", None, None), P("dom", None, None), P(None, "band"), P())
    out_specs = P("band", "dom", None, None)
    return jax.shard_map(
        on_device, mesh=mesh, in_specs=in_specs, out_specs=out_specs, check_vma=False
    )
```

```python
import functools

import jax
import jax.numpy as jnp
import ml_dtypes
import numpy as np
from jax import lax
from jax.experimental import pallas as pl
from jax.experimental.pallas import tpu as pltpu
from jax.sharding import PartitionSpec as P

DEG = 4
RIM = 6
WEIGHTS = (
    -5369.0 / 1800.0,
    12.0 / 7.0,
    -15.0 / 56.0,
    10.0 / 189.0,
    -1.0 / 112.0,
    2.0 / 1925.0,
    -1.0 / 16632.0,
)
CENTER = 8.0
HALF_WIDTH = 5.0
LAPLACE = -1.0 / HALF_WIDTH
SLOPE = 2.0 / HALF_WIDTH
SHIFT = -2.0 * CENTER / HALF_WIDTH + LAPLACE * 3.0 * WEIGHTS[0]
SPAN = [LAPLACE * w for w in WEIGHTS]
GROUP = 4


def band_matrix(size, copies):
    one = np.zeros((size, size), np.float64)
    for offset in range(1, RIM + 1):
        one += SPAN[offset] * (np.eye(size, k=offset) + np.eye(size, k=-offset))
    return np.kron(np.eye(copies), one).astype(np.float32)


def halves(matrix):
    high = matrix.astype(ml_dtypes.bfloat16)
    low = (matrix - high.astype(np.float32)).astype(ml_dtypes.bfloat16)
    return high, low


def second_differences(
    planes, y_ref, odd_ref, even_ref, place, last, pot_ref, mz_ref, my_ref, prev_ref, next_ref
):
    rows, lanes = y_ref.shape[1:]

    def along_plane(g, carry):
        group = pl.ds(pl.multiple_of(g * GROUP, GROUP), GROUP)
        block = y_ref[group].reshape(GROUP * rows, lanes)
        high = block.astype(jnp.bfloat16)
        low = (block - high.astype(jnp.float32)).astype(jnp.bfloat16)
        total = jnp.dot(
            jnp.concatenate([high, high, low], axis=1),
            mz_ref[...],
            preferred_element_type=jnp.float32,
        )
        total = total + jnp.dot(
            my_ref[...],
            jnp.concatenate([high, low, high], axis=0),
            preferred_element_type=jnp.float32,
        )
        next_ref[group] = total.reshape(GROUP, rows, lanes)
        return carry

    lax.fori_loop(0, planes // GROUP, along_plane, 0, unroll=6)

    even = (place & 1) == 0
    zero = jnp.zeros((8, 128), jnp.float32)

    def across_planes(i, carry):
        row = pl.ds(pl.multiple_of(i * 8, 8), 8)
        for j in range(lanes // 128):
            col = pl.ds(j * 128, 128)
            one = [odd_ref[p, row, col] for p in range(RIM)]
            two = [even_ref[p, row, col] for p in range(RIM)]
            line = [jnp.where(place == 0, zero, jnp.where(even, t, o)) for o, t in zip(one, two)]
            line += [y_ref[p, row, col] for p in range(planes)]
            line += [jnp.where(place == last, zero, jnp.where(even, o, t)) for o, t in zip(one, two)]
            for p in range(planes):
                here = p + RIM
                out = next_ref[p, row, col]
                for offset in range(1, RIM + 1):
                    out = out + SPAN[offset] * (line[here - offset] + line[here + offset])
                out = out + (SLOPE * pot_ref[p, row, col] + SHIFT) * line[here]
                if prev_ref is None:
                    next_ref[p, row, col] = 0.5 * out
                else:
                    next_ref[p, row, col] = out - prev_ref[p, row, col]
        return carry

    lax.fori_loop(0, rows // 8, across_planes, 0)


def step_kernel(first, final, place_ref, *refs):
    y_ref, odd_ref, even_ref = refs[:3]
    prev_ref = None if first else refs[3]
    refs = refs[3:] if first else refs[4:]
    pot_ref, mz_ref, my_ref, token_ref = refs[:4]
    planes = y_ref.shape[0]
    place = place_ref[0]
    even = (place & 1) == 0
    last = place_ref[1]
    use = (y_ref, odd_ref, even_ref, place, last, pot_ref, mz_ref, my_ref, prev_ref)

    if final:
        out_ref, next_ref, sems = refs[4:7]
        copies = [pltpu.make_async_copy(token_ref, out_ref.at[0], sems.at[0])]
        copies += [pltpu.make_async_copy(next_ref, out_ref.at[1], sems.at[1])]
        copies[0].start()
        second_differences(planes, *use, next_ref)
        copies[1].start()
        copies[0].wait()
        copies[1].wait()
        return

    next_ref = refs[4]
    second_differences(planes, *use, next_ref)
    if len(refs) == 5:
        return
    near_ref, far_ref = refs[5:7]

    @pl.when(even)
    def _():
        near_ref[...] = next_ref[planes - RIM :]
        far_ref[...] = next_ref[:RIM]

    @pl.when(jnp.logical_not(even))
    def _():
        near_ref[...] = next_ref[:RIM]
        far_ref[...] = next_ref[planes - RIM :]


def step(k, final, place, y, one, two, prev, potential, mz, my, token):
    first = k == 0
    args = [y, one, two] + ([] if first else [prev]) + [potential, mz, my]
    vmem = pl.BlockSpec(memory_space=pltpu.VMEM)
    hbm = pl.BlockSpec(memory_space=pl.ANY)
    rim = jax.ShapeDtypeStruct((RIM,) + y.shape[1:], jnp.float32)
    whole = jax.ShapeDtypeStruct(y.shape, jnp.float32)
    scratch = []
    if final:
        shapes, specs = jax.ShapeDtypeStruct((2,) + y.shape, jnp.float32), hbm
        scratch = [pltpu.VMEM(y.shape, jnp.float32), pltpu.SemaphoreType.DMA((2,))]
    else:
        shapes = (whole,) if k == DEG - 1 else (whole, rim, rim)
        specs = (vmem,) * len(shapes)
    return pl.pallas_call(
        functools.partial(step_kernel, first, final),
        out_shape=shapes,
        in_specs=[pl.BlockSpec(memory_space=pltpu.SMEM)] + [vmem] * len(args) + [hbm],
        out_specs=specs,
        scratch_shapes=scratch,
        compiler_params=pltpu.CompilerParams(vmem_limit_bytes=8 * 1024 * 1024),
        name="chebyshev_first" if first else "chebyshev_step",
    )(place, *args, token)


def blend(turn_ref, states_ref, part_ref, spot, p, row, count):
    panel = [part_ref[s, p, row, :] for s in range(count)]
    for t in range(count):
        total = states_ref[t, spot + p, row, :]
        for s in range(count):
            total = total + turn_ref[s, t] * panel[s]
        yield t, total


def rim_kernel(spots_ref, turn_ref, states_ref, *refs):
    parts, outs, rims_ref = refs[:4], refs[4:-1], refs[-1]
    count = states_ref.shape[0]
    width, rows = parts[0].shape[1:3]
    even = (spots_ref[12] & 1) == 0
    for k in range(4):
        spot, where = spots_ref[k], spots_ref[4 + k]

        def along(i, carry):
            row = pl.ds(pl.multiple_of(i * 8, 8), 8)
            for p in range(width):
                for t, total in blend(turn_ref, states_ref, parts[k], spot, p, row, count):
                    rims_ref[t, where + p, row, :] = total
            return carry

        lax.fori_loop(0, rows // 8, along, 0)

    for t in range(count):
        outs[2 * t][...] = rims_ref[t, :RIM]
        outs[2 * t + 1][...] = rims_ref[t, RIM:]


def body_kernel(spots_ref, turn_ref, states_ref, *refs):
    parts, rims, outs = refs[:4], refs[4:-2], refs[-2:]
    count, planes = states_ref.shape[:2]
    width, rows = parts[0].shape[1:3]
    for k in range(4):
        spot = spots_ref[8 + k]

        def along(i, carry):
            row = pl.ds(pl.multiple_of(i * 8, 8), 8)
            for p in range(width):
                for t, total in blend(turn_ref, states_ref, parts[k], spot, p, row, count):
                    outs[t][spot + p, row, :] = total
            return carry

        lax.fori_loop(0, rows // 8, along, 0)

    even = (spots_ref[12] & 1) == 0
    for t in range(count):
        near, far = rims[2 * t], rims[2 * t + 1]

        @pl.when(even)
        def _():
            outs[t][planes - RIM :] = near[...]
            outs[t][:RIM] = far[...]

        @pl.when(jnp.logical_not(even))
        def _():
            outs[t][:RIM] = near[...]
            outs[t][planes - RIM :] = far[...]


def mixed(kernel, name, spots, turn, states, args, shapes, scratch):
    vmem = pl.BlockSpec(memory_space=pltpu.VMEM)
    smem = pl.BlockSpec(memory_space=pltpu.SMEM)
    return pl.pallas_call(
        kernel,
        out_shape=[jax.ShapeDtypeStruct(s, jnp.float32) for s in shapes],
        in_specs=[smem, smem] + [vmem] * (1 + len(args)),
        out_specs=[vmem] * len(shapes),
        scratch_shapes=scratch,
        compiler_params=pltpu.CompilerParams(vmem_limit_bytes=8 * 1024 * 1024),
        name=name,
    )(spots, turn, states, *args)


def on_device(states, potential, rotation_panel, owner):
    size = lax.axis_size("dom")
    pairs = [(i, i ^ 1) for i in range(size)]
    others = [(i, (i + 1) % size if i % 2 else (i - 1) % size) for i in range(size)]
    depth = lax.axis_size("band") // 4
    count, planes, rows, lanes = states.shape

    def device(x, z, c):
        return (x * depth + z) * 2 + c

    chips = [(x, z, c) for x in range(2) for z in range(depth) for c in range(2)]
    swap_core = [(device(x, z, c), device(x, z, 1 - c)) for x, z, c in chips]
    swap_x = [(device(x, z, c), device(1 - x, z, c)) for x, z, c in chips]

    def shift(k):
        return [(device(x, z, c), device(x, (z + k) % depth, c)) for x, z, c in chips]

    mz_high, mz_low = halves(band_matrix(lanes, 1))
    my_high, my_low = halves(band_matrix(rows, GROUP))
    mz = jnp.asarray(np.concatenate([mz_high, mz_low, mz_high], axis=0))
    my = jnp.asarray(np.concatenate([my_high, my_high, my_low], axis=1))

    me = lax.axis_index("band")
    source = owner[0]
    away = me ^ source
    core_off = away & 1
    x_off = jnp.where(away >= 2 * depth, 1, 0)
    far_z = ((me >> 1) - (source >> 1)) & (depth - 1)
    slab = lax.axis_index("dom")
    place = jnp.stack([slab, jnp.int32(size - 1)])
    odd = slab & 1

    width = RIM // 2
    quarters = [(core_off ^ c) * 2 + (x_off ^ x) for c in (0, 1) for x in (0, 1)]
    rim_spots = [jnp.where(q >= 2, planes - RIM, 0) + width * (q & 1) for q in quarters]
    rim_slots = [RIM * (1 - ((q >> 1) ^ odd)) + width * (q & 1) for q in quarters]
    body_spots = [RIM + width * q for q in quarters]
    spots = jnp.stack(rim_spots + rim_slots + body_spots + [slab])

    def gather(keep, send):
        swapped = lax.ppermute(send, "band", swap_core)
        near = core_off == 0
        stay = jnp.where(near, keep[:, :width], swapped[:, :width])
        pass_on = jnp.where(near, keep[:, width:], swapped[:, width:])
        got = lax.ppermute(pass_on, "band", swap_x)
        return jnp.where(x_off == 0, stay, got), swapped

    middle = planes // 2
    chunk, swapped = gather(states[:, :RIM], states[:, planes - RIM :])
    later, _ = lax.optimization_barrier((states, swapped))
    chunks = [chunk, gather(later[:, RIM:middle], later[:, middle : planes - RIM])[0]]
    rising = far_z <= depth // 2
    hops = jnp.where(rising, far_z, depth - far_z)

    def share(here, there):
        return [
            here,
            there,
            lax.ppermute(here, "band", swap_core),
            lax.ppermute(there, "band", swap_core),
        ]

    stages, arrived = [chunks[0]], list(chunks)
    for stage in range(1, len(chunks) + depth // 2):
        sent = stages[-1]
        up = lax.ppermute(sent, "band", shift(1))
        down = lax.ppermute(sent, "band", shift(-1))
        here = jnp.where(rising, up, down)
        if stage < len(chunks):
            here = jnp.where(hops == 0, chunks[stage], here)
        stages.append(here)
        for c in range(len(chunks)):
            h = stage - c
            if h == 0:
                arrived[c] = here
            elif 0 < h <= depth // 2:
                arrived[c] = jnp.where(hops == h, here, arrived[c])

    here = arrived[0]
    rim_parts = share(here, lax.ppermute(here, "band", swap_x))
    rim_shape = (RIM, rows, lanes)
    rims = mixed(
        rim_kernel, "mix_rims", spots, rotation_panel, states, rim_parts,
        [rim_shape] * (2 * count), [pltpu.VMEM((count, 2 * RIM, rows, lanes), jnp.float32)],
    )
    edges = [(rims[2 * s], rims[2 * s + 1]) for s in range(count)]
    here = arrived[1]
    body_parts = share(here, lax.ppermute(here, "band", swap_x))
    current = list(mixed(
        body_kernel, "mix_body", spots, rotation_panel, states, [*body_parts, *rims],
        [(planes, rows, lanes)] * count, [],
    ))
    previous = [None] * count
    token = potential
    for k in range(DEG):
        for s in range(count):
            one = lax.ppermute(edges[s][0], "dom", pairs)
            two = lax.ppermute(edges[s][1], "dom", others)
            if k == 0 and s == 0:
                edges[1], one, two, *current = lax.optimization_barrier((edges[1], one, two, *current))
            final = k == DEG - 1 and s == count - 1
            out = step(
                k, final, place, current[s], one, two, previous[s], potential, mz, my, token
            )
            if final:
                return out
            previous[s], current[s] = current[s], out[0]
            token = out[1] if k < DEG - 1 else out[0]
            edges[s] = out[1:]


def solution(mesh):
    in_specs = (P("band", "dom", None, None), P("dom", None, None), P(None, "band"), P())
    out_specs = P("band", "dom", None, None)
    return jax.shard_map(
        on_device, mesh=mesh, in_specs=in_specs, out_specs=out_specs, check_vma=False
    )
```

```python
import functools

import jax
import jax.numpy as jnp
import ml_dtypes
import numpy as np
from jax import lax
from jax.experimental import pallas as pl
from jax.experimental.pallas import tpu as pltpu
from jax.sharding import PartitionSpec as P

DEG = 4
RIM = 6
WEIGHTS = (
    -5369.0 / 1800.0,
    12.0 / 7.0,
    -15.0 / 56.0,
    10.0 / 189.0,
    -1.0 / 112.0,
    2.0 / 1925.0,
    -1.0 / 16632.0,
)
CENTER = 8.0
HALF_WIDTH = 5.0
LAPLACE = -1.0 / HALF_WIDTH
SLOPE = 2.0 / HALF_WIDTH
SHIFT = -2.0 * CENTER / HALF_WIDTH + LAPLACE * 3.0 * WEIGHTS[0]
SPAN = [LAPLACE * w for w in WEIGHTS]
GROUP = 4


def band_matrix(size, copies):
    one = np.zeros((size, size), np.float64)
    for offset in range(1, RIM + 1):
        one += SPAN[offset] * (np.eye(size, k=offset) + np.eye(size, k=-offset))
    return np.kron(np.eye(copies), one).astype(np.float32)


def halves(matrix):
    high = matrix.astype(ml_dtypes.bfloat16)
    low = (matrix - high.astype(np.float32)).astype(ml_dtypes.bfloat16)
    return high, low


def second_differences(
    planes, y_ref, odd_ref, even_ref, place, last, pot_ref, mz_ref, my_ref, prev_ref, next_ref
):
    rows, lanes = y_ref.shape[1:]

    def along_plane(g, carry):
        group = pl.ds(pl.multiple_of(g * GROUP, GROUP), GROUP)
        block = y_ref[group].reshape(GROUP * rows, lanes)
        high = block.astype(jnp.bfloat16)
        low = (block - high.astype(jnp.float32)).astype(jnp.bfloat16)
        total = jnp.dot(
            jnp.concatenate([high, high, low], axis=1),
            mz_ref[...],
            preferred_element_type=jnp.float32,
        )
        total = total + jnp.dot(
            my_ref[...],
            jnp.concatenate([high, low, high], axis=0),
            preferred_element_type=jnp.float32,
        )
        next_ref[group] = total.reshape(GROUP, rows, lanes)
        return carry

    lax.fori_loop(0, planes // GROUP, along_plane, 0, unroll=6)

    even = (place & 1) == 0
    zero = jnp.zeros((8, 128), jnp.float32)

    def across_planes(i, carry):
        row = pl.ds(pl.multiple_of(i * 8, 8), 8)
        for j in range(lanes // 128):
            col = pl.ds(j * 128, 128)
            one = [odd_ref[p, row, col] for p in range(RIM)]
            two = [even_ref[p, row, col] for p in range(RIM)]
            line = [jnp.where(place == 0, zero, jnp.where(even, t, o)) for o, t in zip(one, two)]
            line += [y_ref[p, row, col] for p in range(planes)]
            line += [jnp.where(place == last, zero, jnp.where(even, o, t)) for o, t in zip(one, two)]
            for p in range(planes):
                here = p + RIM
                out = next_ref[p, row, col]
                for offset in range(1, RIM + 1):
                    out = out + SPAN[offset] * (line[here - offset] + line[here + offset])
                out = out + (SLOPE * pot_ref[p, row, col] + SHIFT) * line[here]
                if prev_ref is None:
                    next_ref[p, row, col] = 0.5 * out
                else:
                    next_ref[p, row, col] = out - prev_ref[p, row, col]
        return carry

    lax.fori_loop(0, rows // 8, across_planes, 0)


def step_kernel(first, final, place_ref, *refs):
    y_ref, odd_ref, even_ref = refs[:3]
    prev_ref = None if first else refs[3]
    refs = refs[3:] if first else refs[4:]
    pot_ref, mz_ref, my_ref, token_ref = refs[:4]
    planes = y_ref.shape[0]
    place = place_ref[0]
    even = (place & 1) == 0
    last = place_ref[1]
    use = (y_ref, odd_ref, even_ref, place, last, pot_ref, mz_ref, my_ref, prev_ref)

    if final:
        out_ref, next_ref, sems = refs[4:7]
        copies = [pltpu.make_async_copy(token_ref, out_ref.at[0], sems.at[0])]
        copies += [pltpu.make_async_copy(next_ref, out_ref.at[1], sems.at[1])]
        copies[0].start()
        second_differences(planes, *use, next_ref)
        copies[1].start()
        copies[0].wait()
        copies[1].wait()
        return

    next_ref = refs[4]
    second_differences(planes, *use, next_ref)
    if len(refs) == 5:
        return
    near_ref, far_ref = refs[5:7]

    @pl.when(even)
    def _():
        near_ref[...] = next_ref[planes - RIM :]
        far_ref[...] = next_ref[:RIM]

    @pl.when(jnp.logical_not(even))
    def _():
        near_ref[...] = next_ref[:RIM]
        far_ref[...] = next_ref[planes - RIM :]


def step(k, final, place, y, one, two, prev, potential, mz, my, token):
    first = k == 0
    args = [y, one, two] + ([] if first else [prev]) + [potential, mz, my]
    vmem = pl.BlockSpec(memory_space=pltpu.VMEM)
    hbm = pl.BlockSpec(memory_space=pl.ANY)
    rim = jax.ShapeDtypeStruct((RIM,) + y.shape[1:], jnp.float32)
    whole = jax.ShapeDtypeStruct(y.shape, jnp.float32)
    scratch = []
    if final:
        shapes, specs = jax.ShapeDtypeStruct((2,) + y.shape, jnp.float32), hbm
        scratch = [pltpu.VMEM(y.shape, jnp.float32), pltpu.SemaphoreType.DMA((2,))]
    else:
        shapes = (whole,) if k == DEG - 1 else (whole, rim, rim)
        specs = (vmem,) * len(shapes)
    return pl.pallas_call(
        functools.partial(step_kernel, first, final),
        out_shape=shapes,
        in_specs=[pl.BlockSpec(memory_space=pltpu.SMEM)] + [vmem] * len(args) + [hbm],
        out_specs=specs,
        scratch_shapes=scratch,
        compiler_params=pltpu.CompilerParams(vmem_limit_bytes=8 * 1024 * 1024),
        name="chebyshev_first" if first else "chebyshev_step",
    )(place, *args, token)


def blend(turn_ref, states_ref, part_ref, spot, p, row, count):
    panel = [part_ref[s, p, row, :] for s in range(count)]
    for t in range(count):
        total = states_ref[t, spot + p, row, :]
        for s in range(count):
            total = total + turn_ref[s, t] * panel[s]
        yield t, total


def rim_kernel(spots_ref, turn_ref, states_ref, *refs):
    parts, outs, rims_ref = refs[:4], refs[4:-1], refs[-1]
    count = states_ref.shape[0]
    width, rows = parts[0].shape[1:3]
    even = (spots_ref[12] & 1) == 0
    for k in range(4):
        spot, where = spots_ref[k], spots_ref[4 + k]

        def along(i, carry):
            row = pl.ds(pl.multiple_of(i * 8, 8), 8)
            for p in range(width):
                for t, total in blend(turn_ref, states_ref, parts[k], spot, p, row, count):
                    rims_ref[t, where + p, row, :] = total
            return carry

        lax.fori_loop(0, rows // 8, along, 0)

    for t in range(count):
        outs[2 * t][...] = rims_ref[t, :RIM]
        outs[2 * t + 1][...] = rims_ref[t, RIM:]


def body_kernel(spots_ref, turn_ref, states_ref, *refs):
    parts, rims, outs = refs[:4], refs[4:-2], refs[-2:]
    count, planes = states_ref.shape[:2]
    width, rows = parts[0].shape[1:3]
    for k in range(4):
        spot = spots_ref[8 + k]

        def along(i, carry):
            row = pl.ds(pl.multiple_of(i * 8, 8), 8)
            for p in range(width):
                for t, total in blend(turn_ref, states_ref, parts[k], spot, p, row, count):
                    outs[t][spot + p, row, :] = total
            return carry

        lax.fori_loop(0, rows // 8, along, 0)

    even = (spots_ref[12] & 1) == 0
    for t in range(count):
        near, far = rims[2 * t], rims[2 * t + 1]

        @pl.when(even)
        def _():
            outs[t][planes - RIM :] = near[...]
            outs[t][:RIM] = far[...]

        @pl.when(jnp.logical_not(even))
        def _():
            outs[t][:RIM] = near[...]
            outs[t][planes - RIM :] = far[...]


def mixed(kernel, name, spots, turn, states, args, shapes, scratch):
    vmem = pl.BlockSpec(memory_space=pltpu.VMEM)
    smem = pl.BlockSpec(memory_space=pltpu.SMEM)
    return pl.pallas_call(
        kernel,
        out_shape=[jax.ShapeDtypeStruct(s, jnp.float32) for s in shapes],
        in_specs=[smem, smem] + [vmem] * (1 + len(args)),
        out_specs=[vmem] * len(shapes),
        scratch_shapes=scratch,
        compiler_params=pltpu.CompilerParams(vmem_limit_bytes=8 * 1024 * 1024),
        name=name,
    )(spots, turn, states, *args)


def on_device(states, potential, rotation_panel, owner):
    size = lax.axis_size("dom")
    pairs = [(i, i ^ 1) for i in range(size)]
    others = [(i, (i + 1) % size if i % 2 else (i - 1) % size) for i in range(size)]
    depth = lax.axis_size("band") // 4
    count, planes, rows, lanes = states.shape

    def device(x, z, c):
        return (x * depth + z) * 2 + c

    chips = [(x, z, c) for x in range(2) for z in range(depth) for c in range(2)]
    swap_core = [(device(x, z, c), device(x, z, 1 - c)) for x, z, c in chips]
    swap_x = [(device(x, z, c), device(1 - x, z, c)) for x, z, c in chips]

    def shift(k):
        return [(device(x, z, c), device(x, (z + k) % depth, c)) for x, z, c in chips]

    mz_high, mz_low = halves(band_matrix(lanes, 1))
    my_high, my_low = halves(band_matrix(rows, GROUP))
    mz = jnp.asarray(np.concatenate([mz_high, mz_low, mz_high], axis=0))
    my = jnp.asarray(np.concatenate([my_high, my_high, my_low], axis=1))

    me = lax.axis_index("band")
    source = owner[0]
    away = me ^ source
    core_off = away & 1
    x_off = jnp.where(away >= 2 * depth, 1, 0)
    far_z = ((me >> 1) - (source >> 1)) & (depth - 1)
    slab = lax.axis_index("dom")
    place = jnp.stack([slab, jnp.int32(size - 1)])
    odd = slab & 1

    width = RIM // 2
    quarters = [(core_off ^ c) * 2 + (x_off ^ x) for c in (0, 1) for x in (0, 1)]
    rim_spots = [jnp.where(q >= 2, planes - RIM, 0) + width * (q & 1) for q in quarters]
    rim_slots = [RIM * (1 - ((q >> 1) ^ odd)) + width * (q & 1) for q in quarters]
    body_spots = [RIM + width * q for q in quarters]
    spots = jnp.stack(rim_spots + rim_slots + body_spots + [slab])

    def gather(keep, send):
        swapped = lax.ppermute(send, "band", swap_core)
        near = core_off == 0
        stay = jnp.where(near, keep[:, :width], swapped[:, :width])
        pass_on = jnp.where(near, keep[:, width:], swapped[:, width:])
        got = lax.ppermute(pass_on, "band", swap_x)
        return jnp.where(x_off == 0, stay, got), swapped

    middle = planes // 2
    chunk, swapped = gather(states[:, :RIM], states[:, planes - RIM :])
    later, _ = lax.optimization_barrier((states, swapped))
    chunks = [chunk, gather(later[:, RIM:middle], later[:, middle : planes - RIM])[0]]
    rising = far_z <= depth // 2
    hops = jnp.where(rising, far_z, depth - far_z)

    def arrived(c):
        out = stages[c]
        for h in range(1, depth // 2 + 1):
            out = jnp.where(hops == h, stages[c + h], out)
        return out

    def share(here, there):
        return [
            here,
            there,
            lax.ppermute(here, "band", swap_core),
            lax.ppermute(there, "band", swap_core),
        ]

    stages = [chunks[0]]
    for stage in range(1, len(chunks) + depth // 2):
        sent = stages[-1]
        up = lax.ppermute(sent, "band", shift(1))
        down = lax.ppermute(sent, "band", shift(-1))
        here = jnp.where(rising, up, down)
        if stage < len(chunks):
            here = jnp.where(hops == 0, chunks[stage], here)
        stages.append(here)

    here = arrived(0)
    rim_parts = share(here, lax.ppermute(here, "band", swap_x))
    rim_shape = (RIM, rows, lanes)
    rims = mixed(
        rim_kernel, "mix_rims", spots, rotation_panel, states, rim_parts,
        [rim_shape] * (2 * count), [pltpu.VMEM((count, 2 * RIM, rows, lanes), jnp.float32)],
    )
    edges = [(rims[2 * s], rims[2 * s + 1]) for s in range(count)]
    here = arrived(1)
    body_parts = share(here, lax.ppermute(here, "band", swap_x))
    current = list(mixed(
        body_kernel, "mix_body", spots, rotation_panel, states, [*body_parts, *rims],
        [(planes, rows, lanes)] * count, [],
    ))
    previous = [None] * count
    token = potential
    for k in range(DEG):
        for s in range(count):
            one = lax.ppermute(edges[s][0], "dom", pairs)
            two = lax.ppermute(edges[s][1], "dom", others)
            final = k == DEG - 1 and s == count - 1
            out = step(
                k, final, place, current[s], one, two, previous[s], potential, mz, my, token
            )
            if final:
                return out
            previous[s], current[s] = current[s], out[0]
            token = out[1] if k < DEG - 1 else out[0]
            edges[s] = out[1:]


def solution(mesh):
    in_specs = (P("band", "dom", None, None), P("dom", None, None), P(None, "band"), P())
    out_specs = P("band", "dom", None, None)
    return jax.shard_map(
        on_device, mesh=mesh, in_specs=in_specs, out_specs=out_specs, check_vma=False
    )
```
